256 devices in a mesh: blk: 8 (over y, core), ctx: 16 (over x_hi, z), tp: 2 (over x_lo).
Axes of the slice: x: 4 (x_hi: 2, x_lo: 2; x = x_hi * 2 + x_lo), y: 4, z: 8, core: 2. Of those that a mesh axis runs over, the one named last changes fastest.
Arguments:
- query_proj: bfloat16 [16384, 4096], P(('blk', 'ctx'), 'tp'), may hold values from -6 to 6
- key_proj: bfloat16 [16384, 4096], P(('blk', 'ctx'), 'tp'), may hold values from -30 to 30
- value_proj: bfloat16 [16384, 4096], P(('blk', 'ctx'), 'tp'), may hold values from -6 to 6
- output_grad: bfloat16 [16384, 4096], P(('blk', 'ctx'), 'tp'), may hold values from -6 to 6
- long_filter: float32 [2, 2048, 16384], P('tp', ('blk', 'ctx')), may hold values from -0.2 to 0.2
Outputs:
- query_grad: bfloat16 [16384, 4096], P(('blk', 'ctx'), 'tp')
- key_grad: bfloat16 [16384, 4096], P(('blk', 'ctx'), 'tp')
- value_grad: bfloat16 [16384, 4096], P(('blk', 'ctx'), 'tp')
- filter_grad: float32 [2, 2048, 16384], P('tp', ('blk', 'ctx'))
The draws below stay inside these ranges and needn't reach their ends.
All inputs are finite; a program needn't handle non-finite values.
Results may differ from the reference program's by a relative error of at most 0.0085.
Values may be sent and summed in bfloat16 or wider, within the bound.
No kernel may reach another device: no remote copies, remote signals or barrier semaphores. Data moves between devices by JAX's collectives and lax.ppermute only.
A program may use at most 128 MiB of HBM per device.

```python
import math
import jax
import jax.numpy as jnp
from jax import lax

D = 4096
LEN = 16384
CH_TP = 2048


def draw_key_proj(key, part):
    scale_key, jitter_key = jax.random.split(key, 2)
    channel = (jnp.arange(D) % CH_TP).astype(jnp.float32)
    rising = jnp.sqrt(1.0 + 2.0 * channel / max(CH_TP - 1, 1))
    spread = jnp.exp(math.log(10.0) * (jax.random.uniform(scale_key, (D,), jnp.float32) - 0.5))
    scales = 0.8 * rising * spread
    values = scales * jax.random.truncated_normal(jitter_key, -6.0, 6.0, (LEN, D), jnp.float32)
    return values.astype(jnp.bfloat16)


def draw_long_filter(key, part):
    rate_key, shape_key = jax.random.split(key, 2)
    decay = jnp.exp(jax.random.uniform(rate_key, (D // CH_TP, CH_TP, 1), jnp.float32, math.log(0.3), math.log(6.0)))
    position = jnp.arange(LEN, dtype=jnp.float32).reshape(1, 1, LEN) / LEN
    envelope = jnp.exp(-decay * position)
    norming = jnp.sqrt(2.0 * decay / (1.0 - jnp.exp(-2.0 * decay)) / LEN)
    shapes = jax.random.truncated_normal(shape_key, -6.0, 6.0, (D // CH_TP, CH_TP, LEN), jnp.float32)
    return (shapes * envelope * norming).astype(jnp.float32)


def shard_levels(rng, dims, cuts, least, top_value):
    loudness, own = 1.0, jax.random.fold_in(rng, 6)
    for dim, parts in cuts:
        steps = jnp.exp(jax.random.uniform(jax.random.fold_in(own, dim), (parts,), jnp.float32, least / len(cuts), top_value / len(cuts)))
        loudness = loudness * jnp.repeat(steps, dims[dim] // parts).reshape([-1 if axis == dim else 1 for axis in range(len(dims))])
    return loudness


def centred(own_key, dims, scale, most, cuts=(), kind=jnp.bfloat16):
    gain = shard_levels(own_key, dims, cuts, -0.22, 0.18) if cuts else 1.0
    result = jax.random.normal(own_key, dims, jnp.float32) * scale * gain
    return jnp.minimum(jnp.maximum(result, -most), most).astype(kind)


def setup_inputs(seed: int = 0) -> dict:
    arg_keys = jax.random.split(jax.random.key(seed), 6)
    return {
        "query_proj": centred(arg_keys[0], (LEN, D), 1.0, 6.0, ((0, 128), (1, 2))),
        "key_proj": draw_key_proj(jax.random.fold_in(arg_keys[5], 71), 0),
        "value_proj": centred(arg_keys[2], (LEN, D), 1.0, 6.0, ((0, 128), (1, 2))),
        "output_grad": centred(arg_keys[3], (LEN, D), 1.0, 6.0, ((0, 128), (1, 2))),
        "long_filter": draw_long_filter(jax.random.fold_in(arg_keys[5], 71), 0),
    }


def block_grads(pieces):
    gated, gate_part, kernel = pieces
    seq_length = gated.shape[-1]
    padded = 2 * seq_length
    gated_freq = jnp.fft.rfft(gated.astype(jnp.float32), n=padded, axis=-1)
    grad_freq = jnp.fft.rfft(gate_part.astype(jnp.float32), n=padded, axis=-1)
    kernel_freq = jnp.fft.rfft(kernel.astype(jnp.float32), n=padded, axis=-1)
    conv_out = jnp.fft.irfft(gated_freq * kernel_freq, n=padded, axis=-1)[:, :seq_length]
    conv_grad = jnp.fft.irfft(grad_freq * jnp.conj(kernel_freq), n=padded, axis=-1)[:, :seq_length]
    filter_raw = jnp.fft.irfft(grad_freq * jnp.conj(gated_freq), n=padded, axis=-1)[:, :seq_length]
    return (conv_out.astype(jnp.bfloat16), conv_grad.astype(jnp.bfloat16), filter_raw.astype(jnp.float32))

def reference(query_proj, key_proj, value_proj, output_grad, long_filter):
    key_value = (key_proj.astype(jnp.float32) * value_proj.astype(jnp.float32)).astype(jnp.bfloat16)
    gate_grad = (output_grad.astype(jnp.float32) * query_proj.astype(jnp.float32)).astype(jnp.bfloat16)
    group_rows = 256 if D % 256 == 0 else D
    blocks_count = D // group_rows
    kernel = long_filter.reshape(blocks_count, group_rows, LEN)
    stacked = (key_value.T.reshape(blocks_count, group_rows, LEN), gate_grad.T.reshape(blocks_count, group_rows, LEN), kernel)
    conv_out, conv_grad, filter_raw = lax.map(block_grads, stacked)
    conv_rows = conv_out.reshape(D, LEN).T
    grad_rows = conv_grad.reshape(D, LEN).T
    filter_raw = filter_raw.reshape(D, LEN)
    query_grad = (output_grad.astype(jnp.float32) * conv_rows.astype(jnp.float32)).astype(jnp.bfloat16)
    key_grad = (grad_rows.astype(jnp.float32) * value_proj.astype(jnp.float32)).astype(jnp.bfloat16)
    value_grad = (grad_rows.astype(jnp.float32) * key_proj.astype(jnp.float32)).astype(jnp.bfloat16)
    mean_square = jnp.sum(filter_raw * filter_raw) / (D * LEN)
    grad_rms = jnp.sqrt(mean_square + 1e-06)
    factor = jnp.minimum(1.0, 1.0 / grad_rms)
    filter_grad = (filter_raw * factor).reshape(D // CH_TP, CH_TP, LEN)
    return (query_grad, key_grad, value_grad, filter_grad)
```

```python
import math

import jax
import jax.numpy as jnp
import ml_dtypes
import numpy as np
from jax import lax
from jax.experimental import pallas as pl
from jax.experimental.pallas import tpu as pltpu
from jax.sharding import PartitionSpec as P

D = 4096
LEN = 16384
TOK = 128
SRC = 128
CH = 2048
OWN = 16
PAIR = 2 * OWN
ROWS = PAIR + 8
F32 = jnp.float32
BF16 = jnp.bfloat16
SEQ_AXES = ("blk", "ctx")


def two_terms(table):
    high = table.astype(np.float32).astype(ml_dtypes.bfloat16)
    low = (table - high.astype(np.float64)).astype(np.float32).astype(ml_dtypes.bfloat16)
    return high, low


def make_tables():
    i = np.arange(128)
    outer = 2.0 * np.pi * np.outer(i + 0.5, i) / 256.0
    inner = 2.0 * np.pi * np.outer(i, i) / 128.0
    turn = 2.0 * np.pi * np.outer(i + 0.5, i) / (2.0 * LEN)
    cos2, sin2 = np.cos(inner), np.sin(inner)
    w1h, w1l = two_terms(np.concatenate([np.cos(outer), -np.sin(outer)], 0))
    w2h, w2l = two_terms(np.block([[cos2, -sin2], [sin2, cos2]]))
    w3h, _ = two_terms(np.block([[cos2, sin2], [-sin2, cos2]]))
    w4h, _ = two_terms(np.concatenate([np.cos(outer).T, -np.sin(outer).T], 1) / LEN)
    return {
        "w1": np.concatenate([w1h, w1l], 1),
        "w2": w2h,
        "w2l": w2l,
        "w3": w3h,
        "w4": w4h,
        "tc": np.cos(turn).astype(np.float32),
        "ts": np.sin(turn).astype(np.float32),
        "eye": np.eye(256).astype(ml_dtypes.bfloat16),
    }


def mm(left, right):
    return jnp.dot(left, right, preferred_element_type=F32)


def mm_t(left, right):
    return lax.dot_general(left, right, (((1,), (1,)), ((), ())), preferred_element_type=F32)


def product(left, right):
    return (left.astype(F32) * right.astype(F32)).astype(BF16)


def turn_forward(real, imag, tc, ts):
    return real * tc + imag * ts, imag * tc - real * ts


def turn_back(real, imag, tc, ts):
    return real * tc - imag * ts, imag * tc + real * ts


def gate_kernel(q_ref, k_ref, v_ref, g_ref, eye_ref, o_ref):
    eye = eye_ref[...]
    groups = 256 // OWN
    for j in range(q_ref.shape[1] // 256):
        cols = pl.ds(j * 256, 256)
        kv = product(k_ref[:, cols], v_ref[:, cols])
        gg = product(g_ref[:, cols], q_ref[:, cols])
        o_ref[pl.ds(j * groups, groups), :OWN, :] = (
            mm_t(eye, kv).astype(BF16).reshape(groups, OWN, TOK)
        )
        o_ref[pl.ds(j * groups, groups), OWN:, :] = (
            mm_t(eye, gg).astype(BF16).reshape(groups, OWN, TOK)
        )


def gate_call(q, k, v, g, eye):
    width = 512
    tok_spec = pl.BlockSpec((TOK, width), lambda i: (0, i))
    return pl.pallas_call(
        gate_kernel,
        grid=(CH // width,),
        in_specs=[tok_spec] * 4 + [pl.BlockSpec((256, 256), lambda i: (0, 0))],
        out_specs=pl.BlockSpec((width // OWN, PAIR, TOK), lambda i: (i, 0, 0)),
        out_shape=jax.ShapeDtypeStruct((SRC, PAIR, TOK), BF16),
        cost_estimate=pl.CostEstimate(
            flops=4 * 256 * CH * TOK, bytes_accessed=6 * TOK * CH * 2, transcendentals=0
        ),
        name="gate",
    )(q, k, v, g, eye)


def filter_kernel(f_ref, w1_ref, w2_ref, w2l_ref, tc_ref, ts_ref, h_ref, rows):
    for n in range(SRC):
        rows[pl.ds(8 * n, 8), :] = f_ref[0, :, pl.ds(TOK * n, TOK)]

    def step(c, carry):
        data = rows[pl.ds(c, SRC, stride=8), :]
        high = data.astype(BF16)
        low = (data - high.astype(F32)).astype(BF16)
        first = mm(w1_ref[...], jnp.concatenate([high, high], 0)) + mm(w1_ref[:, :128], low)
        real, imag = turn_forward(first[:128], first[128:], tc_ref[...], ts_ref[...])
        mid = jnp.concatenate([real, imag], 1)
        mid_high = mid.astype(BF16)
        mid_low = (mid - mid_high.astype(F32)).astype(BF16)
        h_ref[c] = (
            mm(mid_high, w2_ref[...]) + mm(mid_low, w2_ref[...]) + mm(mid_high, w2l_ref[...])
        )
        return carry

    lax.fori_loop(0, 8, step, 0)


def filter_call(filt, t):
    fixed = lambda a: pl.BlockSpec(a.shape, lambda i: (0, 0))
    tabs = [t[n] for n in ("w1", "w2", "w2l", "tc", "ts")]
    return pl.pallas_call(
        filter_kernel,
        grid=(OWN // 8,),
        in_specs=[pl.BlockSpec((1, 8, LEN), lambda i: (0, i, 0))] + [fixed(a) for a in tabs],
        out_specs=pl.BlockSpec((8, 128, 256), lambda i: (i, 0, 0)),
        out_shape=jax.ShapeDtypeStruct((OWN, 128, 256), F32),
        scratch_shapes=[pltpu.VMEM((8 * SRC, TOK), F32)],
        cost_estimate=pl.CostEstimate(
            flops=OWN * 5 * 2 * 256 * 256 * 128, bytes_accessed=4 << 20, transcendentals=0
        ),
        name="filter_spectrum",
    )(filt, *tabs)


def conv_kernel(
    x_ref, h_ref, w1_ref, w2_ref, w3_ref, w4_ref, tc_ref, ts_ref, o_ref, fr_ref, xf, of, acc
):
    xf[...] = x_ref[...].reshape(SRC * PAIR, TOK).astype(F32)
    acc[...] = jnp.zeros_like(acc)

    def step(c, carry):
        tc, ts = tc_ref[...], ts_ref[...]
        kv = xf[pl.ds(c, SRC, stride=PAIR), :]
        gg = xf[pl.ds(OWN + c, SRC, stride=PAIR), :]
        data = jnp.concatenate([kv, gg], 1).astype(BF16)
        first = mm(w1_ref[...], jnp.concatenate([data, data], 0))
        mid = jnp.concatenate(
            [
                jnp.concatenate(turn_forward(first[:128, :128], first[128:, :128], tc, ts), 1),
                jnp.concatenate(turn_forward(first[:128, 128:], first[128:, 128:], tc, ts), 1),
            ],
            0,
        ).astype(BF16)
        spec = mm(mid, w2_ref[...])
        kr, ki = spec[:128, :128], spec[:128, 128:]
        gr, gi = spec[128:, :128], spec[128:, 128:]
        hr, hi = h_ref[c, :, :128], h_ref[c, :, 128:]
        prod = jnp.concatenate(
            [
                jnp.concatenate([kr * hr - ki * hi, kr * hi + ki * hr], 1),
                jnp.concatenate([gr * hr + gi * hi, gi * hr - gr * hi], 1),
                jnp.concatenate([gr * kr + gi * ki, gi * kr - gr * ki], 1),
            ],
            0,
        ).astype(BF16)
        back = mm(prod, w3_ref[...])
        last = jnp.concatenate(
            [
                jnp.concatenate(
                    turn_back(back[s : s + 128, :128], back[s : s + 128, 128:], tc, ts), 0
                )
                for s in (0, 128, 256)
            ],
            1,
        ).astype(BF16)
        out = mm(w4_ref[...], last)
        of[pl.ds(c, SRC, stride=PAIR), :] = out[:, :128]
        of[pl.ds(OWN + c, SRC, stride=PAIR), :] = out[:, 128:256]
        raw = out[:, 256:]
        fr_ref[pl.ds((c // 8) * (8 * SRC) + c % 8, SRC, stride=8), :] = raw
        acc[...] += jnp.sum((raw * raw).reshape(SRC // 8, 8, TOK), axis=0)
        return carry

    lax.fori_loop(0, OWN, step, 0)
    o_ref[:, :PAIR, :] = of[...].reshape(SRC, PAIR, TOK).astype(BF16)
    total = jnp.broadcast_to(jnp.sum(acc[...]), (8, TOK))
    high = total.astype(BF16).astype(F32)
    mid = (total - high).astype(BF16).astype(F32)
    low = total - high - mid
    row = lax.broadcasted_iota(jnp.int32, (8, TOK), 0)
    terms = jnp.where(row == 0, high, jnp.where(row == 1, mid, jnp.where(row == 2, low, 0.0)))
    o_ref[:, PAIR:, :] = jnp.broadcast_to(terms[None], (SRC, 8, TOK)).astype(BF16)


def conv_call(x, h, t):
    tabs = [t[n] for n in ("w1", "w2", "w3", "w4", "tc", "ts")]
    return pl.pallas_call(
        conv_kernel,
        out_shape=(
            jax.ShapeDtypeStruct((SRC, ROWS, TOK), BF16),
            jax.ShapeDtypeStruct((OWN * SRC, TOK), F32),
        ),
        scratch_shapes=[
            pltpu.VMEM((SRC * PAIR, TOK), F32),
            pltpu.VMEM((SRC * PAIR, TOK), F32),
            pltpu.VMEM((8, TOK), F32),
        ],
        cost_estimate=pl.CostEstimate(
            flops=OWN * 5 * 2 * 256 * 256 * 256, bytes_accessed=6 << 20, transcendentals=0
        ),
        name="conv",
    )(x, h, *tabs)


def stat_kernel(y_ref, o_ref):
    total = jnp.sum(y_ref[...].astype(F32), axis=0)
    o_ref[...] = jnp.broadcast_to(jnp.sum(total[:3], axis=0, keepdims=True), (8, TOK))


def stat_call(y):
    return pl.pallas_call(
        stat_kernel,
        grid=(1,),
        in_specs=[pl.BlockSpec((SRC, 8, TOK), lambda i: (0, PAIR // 8, 0))],
        out_specs=pl.BlockSpec((8, TOK), lambda i: (0, 0)),
        out_shape=jax.ShapeDtypeStruct((8, TOK), F32),
        name="stat",
    )(y)


def token_kernel(y_ref, k_ref, v_ref, g_ref, eye_ref, qg_ref, kg_ref, vg_ref):
    eye = eye_ref[:TOK, :TOK]
    groups = 256 // OWN
    for j in range(k_ref.shape[1] // 256):
        cols = pl.ds(j * 256, 256)
        out = y_ref[pl.ds(j * groups, groups), :OWN, :].reshape(256, TOK)
        grad = y_ref[pl.ds(j * groups, groups), OWN:PAIR, :].reshape(256, TOK)
        conv_out = mm_t(eye, out)
        conv_grad = mm_t(eye, grad)
        qg_ref[:, cols] = (g_ref[:, cols].astype(F32) * conv_out).astype(BF16)
        kg_ref[:, cols] = (v_ref[:, cols].astype(F32) * conv_grad).astype(BF16)
        vg_ref[:, cols] = (k_ref[:, cols].astype(F32) * conv_grad).astype(BF16)


def token_call(y, k, v, g, eye):
    width = 512
    tok_spec = pl.BlockSpec((TOK, width), lambda i: (0, i))
    return pl.pallas_call(
        token_kernel,
        grid=(CH // width,),
        in_specs=[pl.BlockSpec((width // OWN, ROWS, TOK), lambda i: (i, 0, 0))]
        + [tok_spec] * 3
        + [pl.BlockSpec((256, 256), lambda i: (0, 0))],
        out_specs=[tok_spec] * 3,
        out_shape=[jax.ShapeDtypeStruct((TOK, CH), BF16)] * 3,
        cost_estimate=pl.CostEstimate(
            flops=4 * 128 * CH * TOK, bytes_accessed=8 * TOK * CH * 2, transcendentals=0
        ),
        name="token",
    )(y, k, v, g, eye)


def clip_kernel(fr_ref, mine_ref, other_ref, o_ref):
    mean = (mine_ref[...] + other_ref[...]) * (1.0 / (D * LEN))
    rms = jnp.sqrt(mean + 1e-6)
    factor = jnp.minimum(1.0, 1.0 / rms)
    for n in range(fr_ref.shape[0] // 8):
        o_ref[0, :, pl.ds(TOK * n, TOK)] = fr_ref[pl.ds(8 * n, 8), :] * factor


def clip_call(fr, mine, other):
    parts = 2
    step = SRC // parts
    stat = pl.BlockSpec((8, TOK), lambda i, j: (0, 0))
    return pl.pallas_call(
        clip_kernel,
        grid=(OWN // 8, parts),
        in_specs=[pl.BlockSpec((8 * step, TOK), lambda i, j: (i * parts + j, 0)), stat, stat],
        out_specs=pl.BlockSpec((1, 8, step * TOK), lambda i, j: (0, i, j)),
        out_shape=jax.ShapeDtypeStruct((1, OWN, LEN), F32),
        cost_estimate=pl.CostEstimate(flops=1 << 18, bytes_accessed=2 << 20, transcendentals=0),
        name="clip",
    )(fr, mine, other)


def exchange(x):
    return lax.all_to_all(x, SEQ_AXES, split_axis=0, concat_axis=0, tiled=True)


def body(query_proj, key_proj, value_proj, output_grad, long_filter):
    t = {name: jnp.asarray(table) for name, table in make_tables().items()}
    sent = gate_call(query_proj, key_proj, value_proj, output_grad, t["eye"])
    arrived = exchange(sent)
    spectrum = filter_call(long_filter, t)
    back, filter_raw = conv_call(arrived, spectrum, t)
    home = exchange(back)
    mine = stat_call(home)
    other = lax.ppermute(mine, "tp", [(0, 1), (1, 0)])
    query_grad, key_grad, value_grad = token_call(
        home, key_proj, value_proj, output_grad, t["eye"]
    )
    filter_grad = clip_call(filter_raw, mine, other)
    return (query_grad, key_grad, value_grad, filter_grad)


def solution(mesh):
    tokens = P(SEQ_AXES, "tp")
    channels = P("tp", SEQ_AXES, None)
    return jax.shard_map(
        body,
        mesh=mesh,
        in_specs=(tokens, tokens, tokens, tokens, channels),
        out_specs=(tokens, tokens, tokens, channels),
        check_vma=False,
    )
```

```python
import math

import jax
import jax.numpy as jnp
import ml_dtypes
import numpy as np
from jax import lax
from jax.experimental import pallas as pl
from jax.experimental.pallas import tpu as pltpu
from jax.sharding import PartitionSpec as P

D = 4096
LEN = 16384
TOK = 128
SRC = 128
CH = 2048
OWN = 16
PAIR = 2 * OWN
ROWS = PAIR + 8
XS = PAIR + 1
FS = OWN + 1
GROUP = 4
F32 = jnp.float32
BF16 = jnp.bfloat16
SEQ_AXES = ("blk", "ctx")


def two_terms(table):
    high = table.astype(np.float32).astype(ml_dtypes.bfloat16)
    low = (table - high.astype(np.float64)).astype(np.float32).astype(ml_dtypes.bfloat16)
    return high, low


def make_tables():
    i = np.arange(128)
    outer = 2.0 * np.pi * np.outer(i + 0.5, i) / 256.0
    inner = 2.0 * np.pi * np.outer(i, i) / 128.0
    turn = 2.0 * np.pi * np.outer(i + 0.5, i) / (2.0 * LEN)
    cos2, sin2 = np.cos(inner), np.sin(inner)
    w1h, w1l = two_terms(np.concatenate([np.cos(outer), -np.sin(outer)], 0))
    w2h, w2l = two_terms(np.block([[cos2, -sin2], [sin2, cos2]]))
    w4h, _ = two_terms(np.concatenate([np.cos(outer).T, -np.sin(outer).T], 1) / LEN)
    return {
        "w1": np.concatenate([w1h, w1l], 1),
        "w2": w2h,
        "w2l": w2l,
        "w4": w4h,
        "tc": np.cos(turn).astype(np.float32),
        "ts": np.sin(turn).astype(np.float32),
        "eye": np.eye(256).astype(ml_dtypes.bfloat16),
    }


def mm(left, right):
    return jnp.dot(left, right, preferred_element_type=F32)


def mm_t(left, right):
    return lax.dot_general(left, right, (((1,), (1,)), ((), ())), preferred_element_type=F32)


def product(left, right):
    return (left.astype(F32) * right.astype(F32)).astype(BF16)


def turn_forward(real, imag, tc, ts):
    return real * tc + imag * ts, imag * tc - real * ts


def turn_back(real, imag, tc, ts):
    return real * tc - imag * ts, imag * tc + real * ts


HERE = pl.BlockSpec(memory_space=pltpu.VMEM)
THERE = pl.BlockSpec(memory_space=pltpu.HBM)
WIDE = 256
CHUNKS = CH // WIDE
GROUPS = WIDE // OWN
LOADS = 2
STORES = 4


def gate_kernel(q_ref, k_ref, v_ref, g_ref, eye_ref, o_ref, q, k, v, g, out, in_sems, out_sems):
    loads = []
    for h in range(LOADS):
        cols = pl.ds(h * (CH // LOADS), CH // LOADS)
        loads.append(
            [
                pltpu.make_async_copy(src.at[:, cols], dst.at[:, cols], in_sems.at[h, a])
                for a, (src, dst) in enumerate(((k_ref, k), (v_ref, v), (g_ref, g), (q_ref, q)))
            ]
        )
        for load in loads[h]:
            load.start()
    eye = eye_ref[...]
    stores = []
    for j in range(CHUNKS):
        if j % (CHUNKS // LOADS) == 0:
            for load in loads[j // (CHUNKS // LOADS)]:
                load.wait()
        cols = pl.ds(j * WIDE, WIDE)
        rows = pl.ds(j * GROUPS, GROUPS)
        kv = product(k[:, cols], v[:, cols])
        gg = product(g[:, cols], q[:, cols])
        out[rows, :OWN, :] = mm_t(eye, kv).astype(BF16).reshape(GROUPS, OWN, TOK)
        out[rows, OWN:, :] = mm_t(eye, gg).astype(BF16).reshape(GROUPS, OWN, TOK)
        if (j + 1) % (CHUNKS // STORES) == 0:
            p = j // (CHUNKS // STORES)
            rows = pl.ds(p * (SRC // STORES), SRC // STORES)
            stores.append(pltpu.make_async_copy(out.at[rows], o_ref.at[rows], out_sems.at[p]))
            stores[p].start()
    for store in stores:
        store.wait()


def gate_call(q, k, v, g, eye):
    return pl.pallas_call(
        gate_kernel,
        in_specs=[THERE] * 4 + [HERE],
        out_specs=THERE,
        out_shape=jax.ShapeDtypeStruct((SRC, PAIR, TOK), BF16),
        scratch_shapes=[pltpu.VMEM((TOK, CH), BF16)] * 4
        + [
            pltpu.VMEM((SRC, PAIR, TOK), BF16),
            pltpu.SemaphoreType.DMA((LOADS, 4)),
            pltpu.SemaphoreType.DMA((STORES,)),
        ],
        cost_estimate=pl.CostEstimate(
            flops=4 * 256 * CH * TOK, bytes_accessed=6 * TOK * CH * 2, transcendentals=0
        ),
        name="gate",
    )(q, k, v, g, eye)


def filter_kernel(f_ref, w1_ref, w2_ref, w2l_ref, tc_ref, ts_ref, h_hbm, rows, h_ref, sem):
    for n in range(SRC):
        rows[pl.ds(FS * n, OWN), :] = f_ref[0, :, pl.ds(TOK * n, TOK)]

    def step(c, carry):
        data = rows[pl.ds(c, SRC, stride=FS), :]
        high = data.astype(BF16)
        low = (data - high.astype(F32)).astype(BF16)
        first = mm(w1_ref[...], jnp.concatenate([high, high], 0)) + mm(w1_ref[:, :128], low)
        real, imag = turn_forward(first[:128], first[128:], tc_ref[...], ts_ref[...])
        mid = jnp.concatenate([real, imag], 1)
        mid_high = mid.astype(BF16)
        mid_low = (mid - mid_high.astype(F32)).astype(BF16)
        h_ref[c] = (
            mm(mid_high, w2_ref[...]) + mm(mid_low, w2_ref[...]) + mm(mid_high, w2l_ref[...])
        )
        return carry

    lax.fori_loop(0, OWN, step, 0, unroll=2)
    store = pltpu.make_async_copy(h_ref, h_hbm, sem)
    store.start()
    store.wait()


def filter_call(filt, t):
    tabs = [t[n] for n in ("w1", "w2", "w2l", "tc", "ts")]
    return pl.pallas_call(
        filter_kernel,
        in_specs=[HERE] * (1 + len(tabs)),
        out_specs=THERE,
        out_shape=pltpu.HBM((OWN, 128, 256), F32),
        scratch_shapes=[
            pltpu.VMEM((FS * SRC, TOK), F32),
            pltpu.VMEM((OWN, 128, 256), F32),
            pltpu.SemaphoreType.DMA(()),
        ],
        compiler_params=pltpu.CompilerParams(vmem_limit_bytes=12 << 20),
        cost_estimate=pl.CostEstimate(
            flops=OWN * 5 * 2 * 256 * 256 * 128, bytes_accessed=4 << 20, transcendentals=0
        ),
        name="filter_spectrum",
    )(filt, *tabs)


def conv_kernel(
    x_ref, h_hbm, w1_ref, w2_ref, w4_ref, tc_ref, ts_ref, o_ref, ff_hbm,
    h_ref, ff, xf, of, acc, out, sems, h_sem, ff_sem, *bufs
):
    mid_re, mid_im, prod_re, prod_im, last0, last1, last2 = (
        bufs[GROUP * b : GROUP * b + GROUP] for b in range(7)
    )
    h_loads = []
    for j in range(h_sem.shape[0]):
        rows = pl.ds(2 * GROUP * j, 2 * GROUP)
        h_loads.append(pltpu.make_async_copy(h_hbm.at[rows], h_ref.at[rows], h_sem.at[j]))
        h_loads[j].start()
    for n in range(SRC):
        xf[pl.ds(XS * n, PAIR), :] = x_ref[n].astype(F32)
    acc[...] = jnp.zeros_like(acc)
    steps = OWN // GROUP

    def inverse_outer(c, u):
        last = jnp.concatenate([last0[u][...], last1[u][...], last2[u][...]], 1)
        out = mm(w4_ref[...], last)
        of[pl.ds(c, SRC, stride=XS), :] = out[:, :128]
        of[pl.ds(OWN + c, SRC, stride=XS), :] = out[:, 128:256]
        raw = out[:, 256:]
        ff[pl.ds(c, SRC, stride=FS), :] = raw
        acc[...] += jnp.sum((raw * raw).reshape(SRC // 8, 8, TOK), axis=0)

    def inverse_inner(u):
        tc, ts = tc_ref[...], ts_ref[...]
        back = mm_t(jnp.concatenate([prod_re[u][...], prod_im[u][...]], 1), w2_ref[...])
        for s, last in enumerate((last0[u], last1[u], last2[u])):
            rows = slice(128 * s, 128 * s + 128)
            real, imag = turn_back(back[rows, :128], back[rows, 128:], tc, ts)
            last[:128] = real.astype(BF16)
            last[128:] = imag.astype(BF16)

    def forward_inner(c, u):
        spec = mm(jnp.concatenate([mid_re[u][...], mid_im[u][...]], 1), w2_ref[...])
        kr, ki = spec[:128, :128], spec[:128, 128:]
        gr, gi = spec[128:, :128], spec[128:, 128:]
        hr, hi = h_ref[c, :, :128], h_ref[c, :, 128:]
        prod_re[u][:128] = (kr * hr - ki * hi).astype(BF16)
        prod_im[u][:128] = (kr * hi + ki * hr).astype(BF16)
        prod_re[u][128:256] = (gr * hr + gi * hi).astype(BF16)
        prod_im[u][128:256] = (gi * hr - gr * hi).astype(BF16)
        prod_re[u][256:] = (gr * kr + gi * ki).astype(BF16)
        prod_im[u][256:] = (gi * kr - gr * ki).astype(BF16)

    def forward_outer(c, u):
        tc, ts = tc_ref[...], ts_ref[...]
        kv = xf[pl.ds(c, SRC, stride=XS), :].astype(BF16)
        gg = xf[pl.ds(OWN + c, SRC, stride=XS), :].astype(BF16)
        data = jnp.concatenate([kv, gg], 1)
        first = mm(w1_ref[...], jnp.concatenate([data, data], 0))
        for s in range(2):
            rows = slice(128 * s, 128 * s + 128)
            real, imag = turn_forward(first[:128, rows], first[128:, rows], tc, ts)
            mid_re[u][rows] = real.astype(BF16)
            mid_im[u][rows] = imag.astype(BF16)

    for i in range(steps + 3):
        if 0 <= i - 3 < steps:
            for u in range(GROUP):
                inverse_outer(GROUP * (i - 3) + u, u)
        if 0 <= i - 2 < steps:
            for u in range(GROUP):
                inverse_inner(u)
        if 0 <= i - 1 < steps:
            if (i - 1) % 2 == 0:
                h_loads[(i - 1) // 2].wait()
            for u in range(GROUP):
                forward_inner(GROUP * (i - 1) + u, u)
        if i < steps:
            for u in range(GROUP):
                forward_outer(GROUP * i + u, u)
    ff_store = pltpu.make_async_copy(ff, ff_hbm, ff_sem)
    ff_store.start()
    total = jnp.broadcast_to(jnp.sum(acc[...]), (8, TOK))
    high = total.astype(BF16).astype(F32)
    mid = (total - high).astype(BF16).astype(F32)
    low = total - high - mid
    row = lax.broadcasted_iota(jnp.int32, (8, TOK), 0)
    terms = jnp.where(row == 0, high, jnp.where(row == 1, mid, jnp.where(row == 2, low, 0.0)))
    terms = jnp.broadcast_to(terms[None], (SRC, 8, TOK)).astype(BF16)
    parts = sems.shape[0]
    stores = []
    for p in range(parts):
        rows = pl.ds(p * (SRC // parts), SRC // parts)
        for n in range(p * (SRC // parts), (p + 1) * (SRC // parts)):
            out[n, :PAIR, :] = of[pl.ds(XS * n, PAIR), :].astype(BF16)
        out[rows, PAIR:, :] = terms[: SRC // parts]
        stores.append(pltpu.make_async_copy(out.at[rows], o_ref.at[rows], sems.at[p]))
        stores[p].start()
    for store in stores:
        store.wait()
    ff_store.wait()


def conv_call(x, h, t):
    tabs = [t[n] for n in ("w1", "w2", "w4", "tc", "ts")]
    return pl.pallas_call(
        conv_kernel,
        in_specs=[HERE, THERE] + [HERE] * len(tabs),
        out_specs=[THERE, THERE],
        out_shape=(
            jax.ShapeDtypeStruct((SRC, ROWS, TOK), BF16),
            pltpu.HBM((SRC * FS, TOK), F32),
        ),
        scratch_shapes=[
            pltpu.VMEM((OWN, 128, 256), F32),
            pltpu.VMEM((SRC * FS, TOK), F32),
            pltpu.VMEM((SRC * XS, TOK), F32),
            pltpu.VMEM((SRC * XS, TOK), F32),
            pltpu.VMEM((8, TOK), F32),
            pltpu.VMEM((SRC, ROWS, TOK), BF16),
            pltpu.SemaphoreType.DMA((4,)),
            pltpu.SemaphoreType.DMA((OWN // (2 * GROUP),)),
            pltpu.SemaphoreType.DMA(()),
        ]
        + [
            pltpu.VMEM((rows, 128), BF16)
            for rows in (256, 256, 384, 384, 256, 256, 256)
            for _ in range(GROUP)
        ],
        compiler_params=pltpu.CompilerParams(vmem_limit_bytes=14 << 20),
        cost_estimate=pl.CostEstimate(
            flops=OWN * 5 * 2 * 256 * 256 * 256, bytes_accessed=6 << 20, transcendentals=0
        ),
        name="conv",
    )(x, h, *tabs)


def arrange_kernel(ff_ref, o_ref):
    for n in range(SRC):
        for b in range(OWN // 8):
            o_ref[pl.ds(8 * b, 8), pl.ds(TOK * n, TOK)] = ff_ref[pl.ds(FS * n + 8 * b, 8), :]


def arrange_call(ff):
    return pl.pallas_call(
        arrange_kernel,
        in_specs=[HERE],
        out_specs=HERE,
        out_shape=jax.ShapeDtypeStruct((OWN, LEN), F32),
        compiler_params=pltpu.CompilerParams(vmem_limit_bytes=8 << 20),
        cost_estimate=pl.CostEstimate(flops=1 << 18, bytes_accessed=2 << 20, transcendentals=0),
        name="arrange",
    )(ff)


def stat_kernel(y_ref, o_ref):
    total = jnp.sum(y_ref[:, PAIR:, :].astype(F32), axis=0)
    o_ref[...] = jnp.broadcast_to(jnp.sum(total[:3], axis=0, keepdims=True), (8, TOK))


def stat_call(y):
    return pl.pallas_call(
        stat_kernel,
        in_specs=[HERE],
        out_specs=HERE,
        out_shape=jax.ShapeDtypeStruct((8, TOK), F32),
        compiler_params=pltpu.CompilerParams(vmem_limit_bytes=4 << 20),
        name="stat",
    )(y)


def token_kernel(
    y_ref, k_ref, v_ref, g_ref, eye_ref, qg_ref, kg_ref, vg_ref, qg, kg, vg, sems
):
    eye = eye_ref[:TOK, :TOK]
    stores = []
    for j in range(CHUNKS):
        cols = pl.ds(j * WIDE, WIDE)
        rows = pl.ds(j * GROUPS, GROUPS)
        conv_out = mm_t(eye, y_ref[rows, :OWN, :].reshape(WIDE, TOK))
        conv_grad = mm_t(eye, y_ref[rows, OWN:PAIR, :].reshape(WIDE, TOK))
        qg[:, cols] = (g_ref[:, cols].astype(F32) * conv_out).astype(BF16)
        kg[:, cols] = (v_ref[:, cols].astype(F32) * conv_grad).astype(BF16)
        vg[:, cols] = (k_ref[:, cols].astype(F32) * conv_grad).astype(BF16)
        for a, (src, dst) in enumerate(((qg, qg_ref), (kg, kg_ref), (vg, vg_ref))):
            store = pltpu.make_async_copy(src.at[:, cols], dst.at[:, cols], sems.at[j, a])
            store.start()
            stores.append(store)
    for store in stores:
        store.wait()


def token_call(y, k, v, g, eye):
    return pl.pallas_call(
        token_kernel,
        in_specs=[HERE] * 5,
        out_specs=[THERE] * 3,
        out_shape=[jax.ShapeDtypeStruct((TOK, CH), BF16)] * 3,
        scratch_shapes=[pltpu.VMEM((TOK, CH), BF16)] * 3
        + [pltpu.SemaphoreType.DMA((CHUNKS, 3))],
        compiler_params=pltpu.CompilerParams(vmem_limit_bytes=12 << 20),
        cost_estimate=pl.CostEstimate(
            flops=4 * 128 * CH * TOK, bytes_accessed=8 * TOK * CH * 2, transcendentals=0
        ),
        name="token",
    )(y, k, v, g, eye)


def clip_kernel(fr_ref, mine_ref, other_ref, o_ref, buf, sems):
    mean = (mine_ref[0:1, 0:1] + other_ref[0:1, 0:1]) * (1.0 / (D * LEN))
    rms = jnp.sqrt(mean + 1e-6)
    factor = jnp.minimum(1.0, 1.0 / rms)
    factor = jnp.broadcast_to(factor, (OWN, TOK))
    parts = sems.shape[0]
    width = LEN // parts
    copies = []
    for p in range(parts):
        for n in range(width // TOK):
            cols = pl.ds(width * p + TOK * n, TOK)
            buf[:, cols] = fr_ref[:, cols] * factor
        cols = pl.ds(width * p, width)
        copy = pltpu.make_async_copy(buf.at[:, cols], o_ref.at[0, :, cols], sems.at[p])
        copy.start()
        copies.append(copy)
    for copy in copies:
        copy.wait()


def clip_call(fr, mine, other):
    return pl.pallas_call(
        clip_kernel,
        in_specs=[HERE] * 3,
        out_specs=THERE,
        out_shape=jax.ShapeDtypeStruct((1, OWN, LEN), F32),
        scratch_shapes=[pltpu.VMEM((OWN, LEN), F32), pltpu.SemaphoreType.DMA((4,))],
        compiler_params=pltpu.CompilerParams(vmem_limit_bytes=8 << 20),
        cost_estimate=pl.CostEstimate(flops=1 << 18, bytes_accessed=2 << 20, transcendentals=0),
        name="clip",
    )(fr, mine, other)


def exchange(x):
    return lax.all_to_all(x, SEQ_AXES, split_axis=0, concat_axis=0, tiled=True)


def body(query_proj, key_proj, value_proj, output_grad, long_filter):
    t = {name: jnp.asarray(table) for name, table in make_tables().items()}
    sent = gate_call(query_proj, key_proj, value_proj, output_grad, t["eye"])
    arrived = exchange(sent)
    spectrum = filter_call(long_filter, t)
    spectrum = pltpu.with_memory_space_constraint(spectrum, pltpu.HBM)
    back, filter_raw = conv_call(arrived, spectrum, t)
    home = exchange(back)
    placed = arrange_call(filter_raw)
    mine = stat_call(home)
    other = lax.ppermute(mine, "tp", [(0, 1), (1, 0)])
    query_grad, key_grad, value_grad = token_call(
        home, key_proj, value_proj, output_grad, t["eye"]
    )
    filter_grad = clip_call(placed, mine, other)
    return (query_grad, key_grad, value_grad, filter_grad)


def solution(mesh):
    tokens = P(SEQ_AXES, "tp")
    channels = P("tp", SEQ_AXES, None)
    return jax.shard_map(
        body,
        mesh=mesh,
        in_specs=(tokens, tokens, tokens, tokens, channels),
        out_specs=(tokens, tokens, tokens, channels),
        check_vma=False,
    )
```

```python
import math

import jax
import jax.numpy as jnp
import ml_dtypes
import numpy as np
from jax import lax
from jax.experimental import pallas as pl
from jax.experimental.pallas import tpu as pltpu
from jax.sharding import PartitionSpec as P

D = 4096
LEN = 16384
TOK = 128
SRC = 128
CH = 2048
OWN = 16
PAIR = 2 * OWN
ROWS = PAIR + 2
HALF = ROWS // 2
XS = PAIR + 1
FS = OWN + 1
GROUP = 4
F32 = jnp.float32
BF16 = jnp.bfloat16
SEQ_AXES = ("blk", "ctx")


def two_terms(table):
    high = table.astype(np.float32).astype(ml_dtypes.bfloat16)
    low = (table - high.astype(np.float64)).astype(np.float32).astype(ml_dtypes.bfloat16)
    return high, low


def make_tables():
    i = np.arange(128)
    outer = 2.0 * np.pi * np.outer(i + 0.5, i) / 256.0
    inner = 2.0 * np.pi * np.outer(i, i) / 128.0
    turn = 2.0 * np.pi * np.outer(i + 0.5, i) / (2.0 * LEN)
    cos2, sin2 = np.cos(inner), np.sin(inner)
    w1h, w1l = two_terms(np.concatenate([np.cos(outer), -np.sin(outer)], 0))
    w2h, w2l = two_terms(np.block([[cos2, -sin2], [sin2, cos2]]))
    w4h, _ = two_terms(np.concatenate([np.cos(outer).T, -np.sin(outer).T], 1) / LEN)
    return {
        "w1": np.concatenate([w1h, w1l], 1),
        "w2": w2h,
        "w2l": w2l,
        "w4": w4h,
        "tc": np.cos(turn).astype(np.float32),
        "ts": np.sin(turn).astype(np.float32),
        "eye": np.eye(256).astype(ml_dtypes.bfloat16),
    }


def mm(left, right):
    return jnp.dot(left, right, preferred_element_type=F32)


def mm_t(left, right):
    return lax.dot_general(left, right, (((1,), (1,)), ((), ())), preferred_element_type=F32)


def product(left, right):
    return (left.astype(F32) * right.astype(F32)).astype(BF16)


def turn_forward(real, imag, tc, ts):
    return real * tc + imag * ts, imag * tc - real * ts


def turn_back(real, imag, tc, ts):
    return real * tc - imag * ts, imag * tc + real * ts


HERE = pl.BlockSpec(memory_space=pltpu.VMEM)
THERE = pl.BlockSpec(memory_space=pltpu.HBM)
WIDE = 256
CHUNKS = CH // WIDE
GROUPS = WIDE // OWN
LOADS = 2
STORES = 4


def gate_kernel(q_ref, k_ref, v_ref, g_ref, eye_ref, o_ref, q, k, v, g, out, in_sems, out_sems):
    loads = []
    for h in range(LOADS):
        cols = pl.ds(h * (CH // LOADS), CH // LOADS)
        loads.append(
            [
                pltpu.make_async_copy(src.at[:, cols], dst.at[:, cols], in_sems.at[h, a])
                for a, (src, dst) in enumerate(((k_ref, k), (v_ref, v), (g_ref, g), (q_ref, q)))
            ]
        )
        for load in loads[h]:
            load.start()
    eye = eye_ref[...]
    stores = []
    for j in range(CHUNKS):
        if j % (CHUNKS // LOADS) == 0:
            for load in loads[j // (CHUNKS // LOADS)]:
                load.wait()
        cols = pl.ds(j * WIDE, WIDE)
        rows = pl.ds(j * GROUPS, GROUPS)
        kv = product(k[:, cols], v[:, cols])
        gg = product(g[:, cols], q[:, cols])
        out[rows, :OWN, :] = mm_t(eye, kv).astype(BF16).reshape(GROUPS, OWN, TOK)
        out[rows, OWN:, :] = mm_t(eye, gg).astype(BF16).reshape(GROUPS, OWN, TOK)
        if (j + 1) % (CHUNKS // STORES) == 0:
            p = j // (CHUNKS // STORES)
            rows = pl.ds(p * (SRC // STORES), SRC // STORES)
            stores.append(pltpu.make_async_copy(out.at[rows], o_ref.at[rows], out_sems.at[p]))
            stores[p].start()
    for store in stores:
        store.wait()


def gate_call(q, k, v, g, eye):
    return pl.pallas_call(
        gate_kernel,
        in_specs=[THERE] * 4 + [HERE],
        out_specs=THERE,
        out_shape=jax.ShapeDtypeStruct((SRC, PAIR, TOK), BF16),
        scratch_shapes=[pltpu.VMEM((TOK, CH), BF16)] * 4
        + [
            pltpu.VMEM((SRC, PAIR, TOK), BF16),
            pltpu.SemaphoreType.DMA((LOADS, 4)),
            pltpu.SemaphoreType.DMA((STORES,)),
        ],
        cost_estimate=pl.CostEstimate(
            flops=4 * 256 * CH * TOK, bytes_accessed=6 * TOK * CH * 2, transcendentals=0
        ),
        name="gate",
    )(q, k, v, g, eye)


def filter_kernel(f_ref, w1_ref, w2_ref, w2l_ref, tc_ref, ts_ref, h_hbm, rows, h_ref, sem):
    for n in range(SRC):
        rows[pl.ds(FS * n, OWN), :] = f_ref[0, :, pl.ds(TOK * n, TOK)]

    def step(c, carry):
        data = rows[pl.ds(c, SRC, stride=FS), :]
        high = data.astype(BF16)
        low = (data - high.astype(F32)).astype(BF16)
        first = mm(w1_ref[...], jnp.concatenate([high, high], 0)) + mm(w1_ref[:, :128], low)
        real, imag = turn_forward(first[:128], first[128:], tc_ref[...], ts_ref[...])
        mid = jnp.concatenate([real, imag], 1)
        mid_high = mid.astype(BF16)
        mid_low = (mid - mid_high.astype(F32)).astype(BF16)
        h_ref[c] = (
            mm(mid_high, w2_ref[...]) + mm(mid_low, w2_ref[...]) + mm(mid_high, w2l_ref[...])
        )
        return carry

    lax.fori_loop(0, OWN, step, 0, unroll=2)
    store = pltpu.make_async_copy(h_ref, h_hbm, sem)
    store.start()
    store.wait()


def filter_call(filt, t):
    tabs = [t[n] for n in ("w1", "w2", "w2l", "tc", "ts")]
    return pl.pallas_call(
        filter_kernel,
        in_specs=[HERE] * (1 + len(tabs)),
        out_specs=THERE,
        out_shape=pltpu.HBM((OWN, 128, 256), F32),
        scratch_shapes=[
            pltpu.VMEM((FS * SRC, TOK), F32),
            pltpu.VMEM((OWN, 128, 256), F32),
            pltpu.SemaphoreType.DMA(()),
        ],
        compiler_params=pltpu.CompilerParams(vmem_limit_bytes=12 << 20),
        cost_estimate=pl.CostEstimate(
            flops=OWN * 5 * 2 * 256 * 256 * 128, bytes_accessed=4 << 20, transcendentals=0
        ),
        name="filter_spectrum",
    )(filt, *tabs)


def conv_kernel(
    x_ref, h_hbm, w1_ref, w2_ref, w4_ref, tc_ref, ts_ref, o_ref, ff_hbm,
    h_ref, ff, xf, of, acc, out, sems, h_sem, ff_sem, *bufs
):
    mid_re, mid_im, prod_re, prod_im, last0, last1, last2 = (
        bufs[GROUP * b : GROUP * b + GROUP] for b in range(7)
    )
    h_loads = []
    for j in range(h_sem.shape[0]):
        rows = pl.ds(2 * GROUP * j, 2 * GROUP)
        h_loads.append(pltpu.make_async_copy(h_hbm.at[rows], h_ref.at[rows], h_sem.at[j]))
        h_loads[j].start()
    for n in range(SRC):
        xf[pl.ds(XS * n, PAIR), :] = x_ref[n].astype(F32)
    acc[...] = jnp.zeros_like(acc)
    steps = OWN // GROUP

    def inverse_outer(c, u):
        last = jnp.concatenate([last0[u][...], last1[u][...], last2[u][...]], 1)
        out = mm(w4_ref[...], last)
        of[pl.ds(c, SRC, stride=XS), :] = out[:, :128]
        of[pl.ds(OWN + c, SRC, stride=XS), :] = out[:, 128:256]
        raw = out[:, 256:]
        ff[pl.ds(c, SRC, stride=FS), :] = raw
        acc[...] += jnp.sum((raw * raw).reshape(SRC // 8, 8, TOK), axis=0)

    def inverse_inner(u):
        tc, ts = tc_ref[...], ts_ref[...]
        back = mm_t(jnp.concatenate([prod_re[u][...], prod_im[u][...]], 1), w2_ref[...])
        for s, last in enumerate((last0[u], last1[u], last2[u])):
            rows = slice(128 * s, 128 * s + 128)
            real, imag = turn_back(back[rows, :128], back[rows, 128:], tc, ts)
            last[:128] = real.astype(BF16)
            last[128:] = imag.astype(BF16)

    def forward_inner(c, u):
        spec = mm(jnp.concatenate([mid_re[u][...], mid_im[u][...]], 1), w2_ref[...])
        kr, ki = spec[:128, :128], spec[:128, 128:]
        gr, gi = spec[128:, :128], spec[128:, 128:]
        hr, hi = h_ref[c, :, :128], h_ref[c, :, 128:]
        prod_re[u][:128] = (kr * hr - ki * hi).astype(BF16)
        prod_im[u][:128] = (kr * hi + ki * hr).astype(BF16)
        prod_re[u][128:256] = (gr * hr + gi * hi).astype(BF16)
        prod_im[u][128:256] = (gi * hr - gr * hi).astype(BF16)
        prod_re[u][256:] = (gr * kr + gi * ki).astype(BF16)
        prod_im[u][256:] = (gi * kr - gr * ki).astype(BF16)

    def forward_outer(c, u):
        tc, ts = tc_ref[...], ts_ref[...]
        kv = xf[pl.ds(c, SRC, stride=XS), :].astype(BF16)
        gg = xf[pl.ds(OWN + c, SRC, stride=XS), :].astype(BF16)
        data = jnp.concatenate([kv, gg], 1)
        first = mm(w1_ref[...], jnp.concatenate([data, data], 0))
        for s in range(2):
            rows = slice(128 * s, 128 * s + 128)
            real, imag = turn_forward(first[:128, rows], first[128:, rows], tc, ts)
            mid_re[u][rows] = real.astype(BF16)
            mid_im[u][rows] = imag.astype(BF16)

    for i in range(steps + 3):
        if 0 <= i - 3 < steps:
            for u in range(GROUP):
                inverse_outer(GROUP * (i - 3) + u, u)
        if 0 <= i - 2 < steps:
            for u in range(GROUP):
                inverse_inner(u)
        if 0 <= i - 1 < steps:
            if (i - 1) % 2 == 0:
                h_loads[(i - 1) // 2].wait()
            for u in range(GROUP):
                forward_inner(GROUP * (i - 1) + u, u)
        if i < steps:
            for u in range(GROUP):
                forward_outer(GROUP * i + u, u)
    ff_store = pltpu.make_async_copy(ff, ff_hbm, ff_sem)
    ff_store.start()
    total = jnp.broadcast_to(jnp.sum(acc[...]), (8, TOK))
    high = total.astype(BF16).astype(F32)
    mid = (total - high).astype(BF16).astype(F32)
    low = total - high - mid
    row = lax.broadcasted_iota(jnp.int32, (2, TOK), 0)
    lane = lax.broadcasted_iota(jnp.int32, (2, TOK), 1)
    high, mid, low = (a[:2] for a in (high, mid, low))
    terms = jnp.where(row == 0, high, jnp.where(lane < 64, mid, low)).astype(BF16)
    parts = sems.shape[0]
    stores = []
    for p in range(parts):
        rows = pl.ds(p * (SRC // parts), SRC // parts)
        for n in range(p * (SRC // parts), (p + 1) * (SRC // parts)):
            out[n, : HALF - 1] = of[pl.ds(XS * n, PAIR), :].astype(BF16).reshape(HALF - 1, 2, TOK)
            out[n, HALF - 1] = terms
        stores.append(pltpu.make_async_copy(out.at[rows], o_ref.at[rows], sems.at[p]))
        stores[p].start()
    for store in stores:
        store.wait()
    ff_store.wait()


def conv_call(x, h, t):
    tabs = [t[n] for n in ("w1", "w2", "w4", "tc", "ts")]
    return pl.pallas_call(
        conv_kernel,
        in_specs=[HERE, THERE] + [HERE] * len(tabs),
        out_specs=[THERE, THERE],
        out_shape=(
            jax.ShapeDtypeStruct((SRC, HALF, 2, TOK), BF16),
            pltpu.HBM((SRC * FS, TOK), F32),
        ),
        scratch_shapes=[
            pltpu.VMEM((OWN, 128, 256), F32),
            pltpu.VMEM((SRC * FS, TOK), F32),
            pltpu.VMEM((SRC * XS, TOK), F32),
            pltpu.VMEM((SRC * XS, TOK), F32),
            pltpu.VMEM((8, TOK), F32),
            pltpu.VMEM((SRC, HALF, 2, TOK), BF16),
            pltpu.SemaphoreType.DMA((4,)),
            pltpu.SemaphoreType.DMA((OWN // (2 * GROUP),)),
            pltpu.SemaphoreType.DMA(()),
        ]
        + [
            pltpu.VMEM((rows, 128), BF16)
            for rows in (256, 256, 384, 384, 256, 256, 256)
            for _ in range(GROUP)
        ],
        compiler_params=pltpu.CompilerParams(vmem_limit_bytes=28 << 20),
        cost_estimate=pl.CostEstimate(
            flops=OWN * 5 * 2 * 256 * 256 * 256, bytes_accessed=6 << 20, transcendentals=0
        ),
        name="conv",
    )(x, h, *tabs)


def arrange_kernel(ff_ref, o_ref):
    for n in range(SRC):
        for b in range(OWN // 8):
            o_ref[pl.ds(8 * b, 8), pl.ds(TOK * n, TOK)] = ff_ref[pl.ds(FS * n + 8 * b, 8), :]


def arrange_call(ff):
    return pl.pallas_call(
        arrange_kernel,
        in_specs=[HERE],
        out_specs=HERE,
        out_shape=jax.ShapeDtypeStruct((OWN, LEN), F32),
        compiler_params=pltpu.CompilerParams(vmem_limit_bytes=8 << 20),
        cost_estimate=pl.CostEstimate(flops=1 << 18, bytes_accessed=2 << 20, transcendentals=0),
        name="arrange",
    )(ff)


def stat_kernel(y_ref, o_ref):
    total = jnp.sum(y_ref[:, HALF - 1, :, :].astype(F32), axis=0)
    total = total[0:1, 0:1] + total[1:2, 0:1] + total[1:2, 64:65]
    o_ref[...] = jnp.broadcast_to(total, (8, TOK))


def stat_call(y):
    return pl.pallas_call(
        stat_kernel,
        in_specs=[HERE],
        out_specs=HERE,
        out_shape=jax.ShapeDtypeStruct((8, TOK), F32),
        compiler_params=pltpu.CompilerParams(vmem_limit_bytes=4 << 20),
        name="stat",
    )(y)


def token_kernel(
    y_ref, k_ref, v_ref, g_ref, eye_ref, qg_ref, kg_ref, vg_ref, qg, kg, vg, sems
):
    eye = eye_ref[:TOK, :TOK]
    stores = []
    for j in range(CHUNKS):
        cols = pl.ds(j * WIDE, WIDE)
        rows = pl.ds(j * GROUPS, GROUPS)
        conv_out = mm_t(eye, y_ref[rows, : OWN // 2].reshape(WIDE, TOK))
        conv_grad = mm_t(eye, y_ref[rows, OWN // 2 : OWN].reshape(WIDE, TOK))
        qg[:, cols] = (g_ref[:, cols].astype(F32) * conv_out).astype(BF16)
        kg[:, cols] = (v_ref[:, cols].astype(F32) * conv_grad).astype(BF16)
        vg[:, cols] = (k_ref[:, cols].astype(F32) * conv_grad).astype(BF16)
        for a, (src, dst) in enumerate(((qg, qg_ref), (kg, kg_ref), (vg, vg_ref))):
            store = pltpu.make_async_copy(src.at[:, cols], dst.at[:, cols], sems.at[j, a])
            store.start()
            stores.append(store)
    for store in stores:
        store.wait()


def token_call(y, k, v, g, eye):
    return pl.pallas_call(
        token_kernel,
        in_specs=[HERE] * 5,
        out_specs=[THERE] * 3,
        out_shape=[jax.ShapeDtypeStruct((TOK, CH), BF16)] * 3,
        scratch_shapes=[pltpu.VMEM((TOK, CH), BF16)] * 3
        + [pltpu.SemaphoreType.DMA((CHUNKS, 3))],
        compiler_params=pltpu.CompilerParams(vmem_limit_bytes=12 << 20),
        cost_estimate=pl.CostEstimate(
            flops=4 * 128 * CH * TOK, bytes_accessed=8 * TOK * CH * 2, transcendentals=0
        ),
        name="token",
    )(y, k, v, g, eye)


def clip_kernel(fr_ref, mine_ref, other_ref, o_ref, buf, sems):
    mean = (mine_ref[0:1, 0:1] + other_ref[0:1, 0:1]) * (1.0 / (D * LEN))
    rms = jnp.sqrt(mean + 1e-6)
    factor = jnp.minimum(1.0, 1.0 / rms)
    factor = jnp.broadcast_to(factor, (OWN, TOK))
    parts = sems.shape[0]
    width = LEN // parts
    copies = []
    for p in range(parts):
        for n in range(width // TOK):
            cols = pl.ds(width * p + TOK * n, TOK)
            buf[:, cols] = fr_ref[:, cols] * factor
        cols = pl.ds(width * p, width)
        copy = pltpu.make_async_copy(buf.at[:, cols], o_ref.at[0, :, cols], sems.at[p])
        copy.start()
        copies.append(copy)
    for copy in copies:
        copy.wait()


def clip_call(fr, mine, other):
    return pl.pallas_call(
        clip_kernel,
        in_specs=[HERE] * 3,
        out_specs=THERE,
        out_shape=jax.ShapeDtypeStruct((1, OWN, LEN), F32),
        scratch_shapes=[pltpu.VMEM((OWN, LEN), F32), pltpu.SemaphoreType.DMA((4,))],
        compiler_params=pltpu.CompilerParams(vmem_limit_bytes=8 << 20),
        cost_estimate=pl.CostEstimate(flops=1 << 18, bytes_accessed=2 << 20, transcendentals=0),
        name="clip",
    )(fr, mine, other)


def exchange(x):
    return lax.all_to_all(x, SEQ_AXES, split_axis=0, concat_axis=0, tiled=True)


def body(query_proj, key_proj, value_proj, output_grad, long_filter):
    t = {name: jnp.asarray(table) for name, table in make_tables().items()}
    sent = gate_call(query_proj, key_proj, value_proj, output_grad, t["eye"])
    arrived = exchange(sent)
    spectrum = filter_call(long_filter, t)
    spectrum = pltpu.with_memory_space_constraint(spectrum, pltpu.HBM)
    back, filter_raw = conv_call(arrived, spectrum, t)
    home = exchange(back)
    placed = arrange_call(filter_raw)
    mine = stat_call(home)
    other = lax.ppermute(mine, "tp", [(0, 1), (1, 0)])
    query_grad, key_grad, value_grad = token_call(
        home, key_proj, value_proj, output_grad, t["eye"]
    )
    filter_grad = clip_call(placed, mine, other)
    return (query_grad, key_grad, value_grad, filter_grad)


def solution(mesh):
    tokens = P(SEQ_AXES, "tp")
    channels = P("tp", SEQ_AXES, None)
    return jax.shard_map(
        body,
        mesh=mesh,
        in_specs=(tokens, tokens, tokens, tokens, channels),
        out_specs=(tokens, tokens, tokens, channels),
        check_vma=False,
    )
```

```python
import math

import jax
import jax.numpy as jnp
import ml_dtypes
import numpy as np
from jax import lax
from jax.experimental import pallas as pl
from jax.experimental.pallas import tpu as pltpu
from jax.sharding import PartitionSpec as P

D = 4096
LEN = 16384
TOK = 128
SRC = 128
CH = 2048
OWN = 16
PAIR = 2 * OWN
ROWS = PAIR + 2
HALF = ROWS // 2
XS = PAIR + 1
FS = OWN + 1
GROUP = 4
F32 = jnp.float32
BF16 = jnp.bfloat16
SEQ_AXES = ("blk", "ctx")


def two_terms(table):
    high = table.astype(np.float32).astype(ml_dtypes.bfloat16)
    low = (table - high.astype(np.float64)).astype(np.float32).astype(ml_dtypes.bfloat16)
    return high, low


def make_tables():
    i = np.arange(128)
    outer = 2.0 * np.pi * np.outer(i + 0.5, i) / 256.0
    inner = 2.0 * np.pi * np.outer(i, i) / 128.0
    turn = 2.0 * np.pi * np.outer(i + 0.5, i) / (2.0 * LEN)
    cos2, sin2 = np.cos(inner), np.sin(inner)
    w1h, w1l = two_terms(np.concatenate([np.cos(outer), -np.sin(outer)], 0))
    w2h, w2l = two_terms(np.block([[cos2, -sin2], [sin2, cos2]]))
    w4h, _ = two_terms(np.concatenate([np.cos(outer).T, -np.sin(outer).T], 1) / LEN)
    return {
        "w1": np.concatenate([w1h, w1l], 1),
        "w2": w2h,
        "w2l": w2l,
        "w4": w4h,
        "tc": np.cos(turn).astype(np.float32),
        "ts": np.sin(turn).astype(np.float32),
        "eye": np.eye(256).astype(ml_dtypes.bfloat16),
    }


def mm(left, right):
    return jnp.dot(left, right, preferred_element_type=F32)


def mm_t(left, right):
    return lax.dot_general(left, right, (((1,), (1,)), ((), ())), preferred_element_type=F32)


def product(left, right):
    return (left.astype(F32) * right.astype(F32)).astype(BF16)


def turn_forward(real, imag, tc, ts):
    return real * tc + imag * ts, imag * tc - real * ts


def turn_back(real, imag, tc, ts):
    return real * tc - imag * ts, imag * tc + real * ts


HERE = pl.BlockSpec(memory_space=pltpu.VMEM)
THERE = pl.BlockSpec(memory_space=pltpu.HBM)
WIDE = 256
CHUNKS = CH // WIDE
GROUPS = WIDE // OWN
LOADS = 2
STORES = 4


def gate_kernel(q_ref, k_ref, v_ref, g_ref, eye_ref, o_ref, q, k, v, g, out, in_sems, out_sems):
    loads = []
    for h in range(LOADS):
        cols = pl.ds(h * (CH // LOADS), CH // LOADS)
        loads.append(
            [
                pltpu.make_async_copy(src.at[:, cols], dst.at[:, cols], in_sems.at[h, a])
                for a, (src, dst) in enumerate(((k_ref, k), (v_ref, v), (g_ref, g), (q_ref, q)))
            ]
        )
        for load in loads[h]:
            load.start()
    eye = eye_ref[...]
    stores = []
    for j in range(CHUNKS):
        if j % (CHUNKS // LOADS) == 0:
            for load in loads[j // (CHUNKS // LOADS)]:
                load.wait()
        cols = pl.ds(j * WIDE, WIDE)
        rows = pl.ds(j * GROUPS, GROUPS)
        kv = product(k[:, cols], v[:, cols])
        gg = product(g[:, cols], q[:, cols])
        out[rows, :OWN, :] = mm_t(eye, kv).astype(BF16).reshape(GROUPS, OWN, TOK)
        out[rows, OWN:, :] = mm_t(eye, gg).astype(BF16).reshape(GROUPS, OWN, TOK)
        if (j + 1) % (CHUNKS // STORES) == 0:
            p = j // (CHUNKS // STORES)
            rows = pl.ds(p * (SRC // STORES), SRC // STORES)
            stores.append(pltpu.make_async_copy(out.at[rows], o_ref.at[rows], out_sems.at[p]))
            stores[p].start()
    for store in stores:
        store.wait()


def gate_call(q, k, v, g, eye):
    return pl.pallas_call(
        gate_kernel,
        in_specs=[THERE] * 4 + [HERE],
        out_specs=THERE,
        out_shape=jax.ShapeDtypeStruct((SRC, PAIR, TOK), BF16),
        scratch_shapes=[pltpu.VMEM((TOK, CH), BF16)] * 4
        + [
            pltpu.VMEM((SRC, PAIR, TOK), BF16),
            pltpu.SemaphoreType.DMA((LOADS, 4)),
            pltpu.SemaphoreType.DMA((STORES,)),
        ],
        cost_estimate=pl.CostEstimate(
            flops=4 * 256 * CH * TOK, bytes_accessed=6 * TOK * CH * 2, transcendentals=0
        ),
        name="gate",
    )(q, k, v, g, eye)


def filter_kernel(f_ref, w1_ref, w2_ref, w2l_ref, tc_ref, ts_ref, h_hbm, rows, h_ref, sem):
    for n in range(SRC):
        rows[pl.ds(FS * n, OWN), :] = f_ref[0, :, pl.ds(TOK * n, TOK)]

    def step(c, carry):
        data = rows[pl.ds(c, SRC, stride=FS), :]
        high = data.astype(BF16)
        low = (data - high.astype(F32)).astype(BF16)
        first = mm(w1_ref[...], jnp.concatenate([high, high], 0)) + mm(w1_ref[:, :128], low)
        real, imag = turn_forward(first[:128], first[128:], tc_ref[...], ts_ref[...])
        mid = jnp.concatenate([real, imag], 1)
        mid_high = mid.astype(BF16)
        mid_low = (mid - mid_high.astype(F32)).astype(BF16)
        h_ref[c] = (
            mm(mid_high, w2_ref[...]) + mm(mid_low, w2_ref[...]) + mm(mid_high, w2l_ref[...])
        )
        return carry

    lax.fori_loop(0, OWN, step, 0, unroll=2)
    store = pltpu.make_async_copy(h_ref, h_hbm, sem)
    store.start()
    store.wait()


def filter_call(filt, t):
    tabs = [t[n] for n in ("w1", "w2", "w2l", "tc", "ts")]
    return pl.pallas_call(
        filter_kernel,
        in_specs=[HERE] * (1 + len(tabs)),
        out_specs=THERE,
        out_shape=pltpu.HBM((OWN, 128, 256), F32),
        scratch_shapes=[
            pltpu.VMEM((FS * SRC, TOK), F32),
            pltpu.VMEM((OWN, 128, 256), F32),
            pltpu.SemaphoreType.DMA(()),
        ],
        compiler_params=pltpu.CompilerParams(vmem_limit_bytes=12 << 20),
        cost_estimate=pl.CostEstimate(
            flops=OWN * 5 * 2 * 256 * 256 * 128, bytes_accessed=4 << 20, transcendentals=0
        ),
        name="filter_spectrum",
    )(filt, *tabs)


def conv_kernel(
    x_ref, h_hbm, w1_ref, w2_ref, w4_ref, tc_ref, ts_ref, o_ref, ff_hbm,
    h_ref, ff, xf, of, acc, out, tail, sems, h_sem, ff_sem, *bufs
):
    mid_re, mid_im, prod_re, prod_im, last0, last1, last2 = (
        bufs[GROUP * b : GROUP * b + GROUP] for b in range(7)
    )
    h_loads = []
    for j in range(h_sem.shape[0]):
        rows = pl.ds(2 * GROUP * j, 2 * GROUP)
        h_loads.append(pltpu.make_async_copy(h_hbm.at[rows], h_ref.at[rows], h_sem.at[j]))
        h_loads[j].start()
    for n in range(SRC):
        xf[pl.ds(XS * n, PAIR), :] = x_ref[n].astype(F32)
    acc[...] = jnp.zeros_like(acc)
    steps = OWN // GROUP

    def inverse_outer(c, u):
        last = jnp.concatenate([last0[u][...], last1[u][...], last2[u][...]], 1)
        out = mm(w4_ref[...], last)
        of[pl.ds(c, SRC, stride=XS), :] = out[:, :128]
        of[pl.ds(OWN + c, SRC, stride=XS), :] = out[:, 128:256]
        raw = out[:, 256:]
        ff[pl.ds(c, SRC, stride=FS), :] = raw
        acc[...] += jnp.sum((raw * raw).reshape(SRC // 8, 8, TOK), axis=0)

    def inverse_inner(u):
        tc, ts = tc_ref[...], ts_ref[...]
        back = mm_t(jnp.concatenate([prod_re[u][...], prod_im[u][...]], 1), w2_ref[...])
        for s, last in enumerate((last0[u], last1[u], last2[u])):
            rows = slice(128 * s, 128 * s + 128)
            real, imag = turn_back(back[rows, :128], back[rows, 128:], tc, ts)
            last[:128] = real.astype(BF16)
            last[128:] = imag.astype(BF16)

    def forward_inner(c, u):
        spec = mm(jnp.concatenate([mid_re[u][...], mid_im[u][...]], 1), w2_ref[...])
        kr, ki = spec[:128, :128], spec[:128, 128:]
        gr, gi = spec[128:, :128], spec[128:, 128:]
        hr, hi = h_ref[c, :, :128], h_ref[c, :, 128:]
        prod_re[u][:128] = (kr * hr - ki * hi).astype(BF16)
        prod_im[u][:128] = (kr * hi + ki * hr).astype(BF16)
        prod_re[u][128:256] = (gr * hr + gi * hi).astype(BF16)
        prod_im[u][128:256] = (gi * hr - gr * hi).astype(BF16)
        prod_re[u][256:] = (gr * kr + gi * ki).astype(BF16)
        prod_im[u][256:] = (gi * kr - gr * ki).astype(BF16)

    def forward_outer(c, u):
        tc, ts = tc_ref[...], ts_ref[...]
        kv = xf[pl.ds(c, SRC, stride=XS), :].astype(BF16)
        gg = xf[pl.ds(OWN + c, SRC, stride=XS), :].astype(BF16)
        data = jnp.concatenate([kv, gg], 1)
        first = mm(w1_ref[...], jnp.concatenate([data, data], 0))
        for s in range(2):
            rows = slice(128 * s, 128 * s + 128)
            real, imag = turn_forward(first[:128, rows], first[128:, rows], tc, ts)
            mid_re[u][rows] = real.astype(BF16)
            mid_im[u][rows] = imag.astype(BF16)

    for i in range(steps + 3):
        if 0 <= i - 3 < steps:
            for u in range(GROUP):
                inverse_outer(GROUP * (i - 3) + u, u)
        if 0 <= i - 2 < steps:
            for u in range(GROUP):
                inverse_inner(u)
        if 0 <= i - 1 < steps:
            if (i - 1) % 2 == 0:
                h_loads[(i - 1) // 2].wait()
            for u in range(GROUP):
                forward_inner(GROUP * (i - 1) + u, u)
        if i < steps:
            for u in range(GROUP):
                forward_outer(GROUP * i + u, u)
    ff_store = pltpu.make_async_copy(ff, ff_hbm, ff_sem)
    ff_store.start()
    total = jnp.broadcast_to(jnp.sum(acc[...]), (8, TOK))
    high = total.astype(BF16).astype(F32)
    mid = (total - high).astype(BF16).astype(F32)
    low = total - high - mid
    row = lax.broadcasted_iota(jnp.int32, (2, TOK), 0)
    lane = lax.broadcasted_iota(jnp.int32, (2, TOK), 1)
    high, mid, low = (a[:2] for a in (high, mid, low))
    terms = jnp.where(row == 0, high, jnp.where(lane < 64, mid, low)).astype(BF16)
    tail[...] = jnp.broadcast_to(terms[None, None], tail.shape)
    parts = sems.shape[0] - 1
    tail_store = pltpu.make_async_copy(tail, o_ref.at[:, HALF - 1 :], sems.at[parts])
    tail_store.start()
    stores = []
    for p in range(parts):
        rows = pl.ds(p * (SRC // parts), SRC // parts)
        for n in range(p * (SRC // parts), (p + 1) * (SRC // parts)):
            out[n] = of[pl.ds(XS * n, PAIR), :].astype(BF16)
        there = o_ref.reshape(SRC, ROWS, TOK).at[rows, :PAIR]
        stores.append(pltpu.make_async_copy(out.at[rows], there, sems.at[p]))
        stores[p].start()
    for store in stores:
        store.wait()
    ff_store.wait()
    tail_store.wait()


def conv_call(x, h, t):
    tabs = [t[n] for n in ("w1", "w2", "w4", "tc", "ts")]
    return pl.pallas_call(
        conv_kernel,
        in_specs=[HERE, THERE] + [HERE] * len(tabs),
        out_specs=[THERE, THERE],
        out_shape=(
            jax.ShapeDtypeStruct((SRC, HALF, 2, TOK), BF16),
            pltpu.HBM((SRC * FS, TOK), F32),
        ),
        scratch_shapes=[
            pltpu.VMEM((OWN, 128, 256), F32),
            pltpu.VMEM((SRC * FS, TOK), F32),
            pltpu.VMEM((SRC * XS, TOK), F32),
            pltpu.VMEM((SRC * XS, TOK), F32),
            pltpu.VMEM((8, TOK), F32),
            pltpu.VMEM((SRC, PAIR, TOK), BF16),
            pltpu.VMEM((SRC, 1, 2, TOK), BF16),
            pltpu.SemaphoreType.DMA((5,)),
            pltpu.SemaphoreType.DMA((OWN // (2 * GROUP),)),
            pltpu.SemaphoreType.DMA(()),
        ]
        + [
            pltpu.VMEM((rows, 128), BF16)
            for rows in (256, 256, 384, 384, 256, 256, 256)
            for _ in range(GROUP)
        ],
        compiler_params=pltpu.CompilerParams(vmem_limit_bytes=28 << 20),
        cost_estimate=pl.CostEstimate(
            flops=OWN * 5 * 2 * 256 * 256 * 256, bytes_accessed=6 << 20, transcendentals=0
        ),
        name="conv",
    )(x, h, *tabs)


def arrange_kernel(ff_ref, o_ref):
    for n in range(SRC):
        for b in range(OWN // 8):
            o_ref[pl.ds(8 * b, 8), pl.ds(TOK * n, TOK)] = ff_ref[pl.ds(FS * n + 8 * b, 8), :]


def arrange_call(ff):
    return pl.pallas_call(
        arrange_kernel,
        in_specs=[HERE],
        out_specs=HERE,
        out_shape=jax.ShapeDtypeStruct((OWN, LEN), F32),
        compiler_params=pltpu.CompilerParams(vmem_limit_bytes=8 << 20),
        cost_estimate=pl.CostEstimate(flops=1 << 18, bytes_accessed=2 << 20, transcendentals=0),
        name="arrange",
    )(ff)


def stat_kernel(y_ref, o_ref):
    total = jnp.sum(y_ref[:, HALF - 1, :, :].astype(F32), axis=0)
    total = total[0:1, 0:1] + total[1:2, 0:1] + total[1:2, 64:65]
    o_ref[...] = jnp.broadcast_to(total, (8, TOK))


def stat_call(y):
    return pl.pallas_call(
        stat_kernel,
        in_specs=[HERE],
        out_specs=HERE,
        out_shape=jax.ShapeDtypeStruct((8, TOK), F32),
        compiler_params=pltpu.CompilerParams(vmem_limit_bytes=4 << 20),
        name="stat",
    )(y)


def token_kernel(
    y_ref, k_ref, v_ref, g_ref, eye_ref, qg_ref, kg_ref, vg_ref, qg, kg, vg, sems
):
    eye = eye_ref[:TOK, :TOK]
    stores = []
    for j in range(CHUNKS):
        cols = pl.ds(j * WIDE, WIDE)
        rows = pl.ds(j * GROUPS, GROUPS)
        conv_out = mm_t(eye, y_ref[rows, : OWN // 2].reshape(WIDE, TOK))
        conv_grad = mm_t(eye, y_ref[rows, OWN // 2 : OWN].reshape(WIDE, TOK))
        qg[:, cols] = (g_ref[:, cols].astype(F32) * conv_out).astype(BF16)
        kg[:, cols] = (v_ref[:, cols].astype(F32) * conv_grad).astype(BF16)
        vg[:, cols] = (k_ref[:, cols].astype(F32) * conv_grad).astype(BF16)
        for a, (src, dst) in enumerate(((qg, qg_ref), (kg, kg_ref), (vg, vg_ref))):
            store = pltpu.make_async_copy(src.at[:, cols], dst.at[:, cols], sems.at[j, a])
            store.start()
            stores.append(store)
    for store in stores:
        store.wait()


def token_call(y, k, v, g, eye):
    return pl.pallas_call(
        token_kernel,
        in_specs=[HERE] * 5,
        out_specs=[THERE] * 3,
        out_shape=[jax.ShapeDtypeStruct((TOK, CH), BF16)] * 3,
        scratch_shapes=[pltpu.VMEM((TOK, CH), BF16)] * 3
        + [pltpu.SemaphoreType.DMA((CHUNKS, 3))],
        compiler_params=pltpu.CompilerParams(vmem_limit_bytes=12 << 20),
        cost_estimate=pl.CostEstimate(
            flops=4 * 128 * CH * TOK, bytes_accessed=8 * TOK * CH * 2, transcendentals=0
        ),
        name="token",
    )(y, k, v, g, eye)


def clip_kernel(fr_ref, mine_ref, other_ref, o_ref, buf, sems):
    mean = (mine_ref[0:1, 0:1] + other_ref[0:1, 0:1]) * (1.0 / (D * LEN))
    rms = jnp.sqrt(mean + 1e-6)
    factor = jnp.minimum(1.0, 1.0 / rms)
    factor = jnp.broadcast_to(factor, (OWN, TOK))
    parts = sems.shape[0]
    width = LEN // parts
    copies = []
    for p in range(parts):
        for n in range(width // TOK):
            cols = pl.ds(width * p + TOK * n, TOK)
            buf[:, cols] = fr_ref[:, cols] * factor
        cols = pl.ds(width * p, width)
        copy = pltpu.make_async_copy(buf.at[:, cols], o_ref.at[0, :, cols], sems.at[p])
        copy.start()
        copies.append(copy)
    for copy in copies:
        copy.wait()


def clip_call(fr, mine, other):
    return pl.pallas_call(
        clip_kernel,
        in_specs=[HERE] * 3,
        out_specs=THERE,
        out_shape=jax.ShapeDtypeStruct((1, OWN, LEN), F32),
        scratch_shapes=[pltpu.VMEM((OWN, LEN), F32), pltpu.SemaphoreType.DMA((4,))],
        compiler_params=pltpu.CompilerParams(vmem_limit_bytes=8 << 20),
        cost_estimate=pl.CostEstimate(flops=1 << 18, bytes_accessed=2 << 20, transcendentals=0),
        name="clip",
    )(fr, mine, other)


def exchange(x):
    return lax.all_to_all(x, SEQ_AXES, split_axis=0, concat_axis=0, tiled=True)


def body(query_proj, key_proj, value_proj, output_grad, long_filter):
    t = {name: jnp.asarray(table) for name, table in make_tables().items()}
    sent = gate_call(query_proj, key_proj, value_proj, output_grad, t["eye"])
    arrived = exchange(sent)
    spectrum = filter_call(long_filter, t)
    spectrum = pltpu.with_memory_space_constraint(spectrum, pltpu.HBM)
    back, filter_raw = conv_call(arrived, spectrum, t)
    home = exchange(back)
    placed = arrange_call(filter_raw)
    mine = stat_call(home)
    other = lax.ppermute(mine, "tp", [(0, 1), (1, 0)])
    query_grad, key_grad, value_grad = token_call(
        home, key_proj, value_proj, output_grad, t["eye"]
    )
    filter_grad = clip_call(placed, mine, other)
    return (query_grad, key_grad, value_grad, filter_grad)


def solution(mesh):
    tokens = P(SEQ_AXES, "tp")
    channels = P("tp", SEQ_AXES, None)
    return jax.shard_map(
        body,
        mesh=mesh,
        in_specs=(tokens, tokens, tokens, tokens, channels),
        out_specs=(tokens, tokens, tokens, channels),
        check_vma=False,
    )
```

```python
import math

import jax
import jax.numpy as jnp
import ml_dtypes
import numpy as np
from jax import lax
from jax.experimental import pallas as pl
from jax.experimental.pallas import tpu as pltpu
from jax.sharding import PartitionSpec as P

D = 4096
LEN = 16384
TOK = 128
SRC = 128
CH = 2048
OWN = 16
PAIR = 2 * OWN
ROWS = PAIR + 2
HALF = ROWS // 2
XS = PAIR + 1
FS = OWN + 1
GROUP = 8
F32 = jnp.float32
BF16 = jnp.bfloat16
SEQ_AXES = ("blk", "ctx")


def two_terms(table):
    high = table.astype(np.float32).astype(ml_dtypes.bfloat16)
    low = (table - high.astype(np.float64)).astype(np.float32).astype(ml_dtypes.bfloat16)
    return high, low


def make_tables():
    i = np.arange(128)
    outer = 2.0 * np.pi * np.outer(i + 0.5, i) / 256.0
    inner = 2.0 * np.pi * np.outer(i, i) / 128.0
    turn = 2.0 * np.pi * np.outer(i + 0.5, i) / (2.0 * LEN)
    cos2, sin2 = np.cos(inner), np.sin(inner)
    w1h, w1l = two_terms(np.concatenate([np.cos(outer), -np.sin(outer)], 0))
    w2h, w2l = two_terms(np.block([[cos2, -sin2], [sin2, cos2]]))
    w4h, _ = two_terms(np.concatenate([np.cos(outer).T, -np.sin(outer).T], 1) / LEN)
    return {
        "w1": np.concatenate([w1h, w1l], 1),
        "w2": w2h,
        "w2l": w2l,
        "w4": w4h,
        "tc": np.cos(turn).astype(np.float32),
        "ts": np.sin(turn).astype(np.float32),
        "eye": np.eye(256).astype(ml_dtypes.bfloat16),
    }


def mm(left, right):
    return jnp.dot(left, right, preferred_element_type=F32)


def mm_t(left, right):
    return lax.dot_general(left, right, (((1,), (1,)), ((), ())), preferred_element_type=F32)


def product(left, right):
    return (left.astype(F32) * right.astype(F32)).astype(BF16)


def turn_forward(real, imag, tc, ts):
    return real * tc + imag * ts, imag * tc - real * ts


def turn_back(real, imag, tc, ts):
    return real * tc - imag * ts, imag * tc + real * ts


HERE = pl.BlockSpec(memory_space=pltpu.VMEM)
THERE = pl.BlockSpec(memory_space=pltpu.HBM)
WIDE = 256
CHUNKS = CH // WIDE
GROUPS = WIDE // OWN
LOADS = 2
STORES = 4


def gate_kernel(q_ref, k_ref, v_ref, g_ref, eye_ref, o_ref, q, k, v, g, out, in_sems, out_sems):
    loads = []
    for h in range(LOADS):
        cols = pl.ds(h * (CH // LOADS), CH // LOADS)
        loads.append(
            [
                pltpu.make_async_copy(src.at[:, cols], dst.at[:, cols], in_sems.at[h, a])
                for a, (src, dst) in enumerate(((k_ref, k), (v_ref, v), (g_ref, g), (q_ref, q)))
            ]
        )
        for load in loads[h]:
            load.start()
    eye = eye_ref[...]
    stores = []
    for j in range(CHUNKS):
        if j % (CHUNKS // LOADS) == 0:
            for load in loads[j // (CHUNKS // LOADS)]:
                load.wait()
        cols = pl.ds(j * WIDE, WIDE)
        rows = pl.ds(j * GROUPS, GROUPS)
        kv = product(k[:, cols], v[:, cols])
        gg = product(g[:, cols], q[:, cols])
        out[rows, :OWN, :] = mm_t(eye, kv).astype(BF16).reshape(GROUPS, OWN, TOK)
        out[rows, OWN:, :] = mm_t(eye, gg).astype(BF16).reshape(GROUPS, OWN, TOK)
        if (j + 1) % (CHUNKS // STORES) == 0:
            p = j // (CHUNKS // STORES)
            rows = pl.ds(p * (SRC // STORES), SRC // STORES)
            stores.append(pltpu.make_async_copy(out.at[rows], o_ref.at[rows], out_sems.at[p]))
            stores[p].start()
    for store in stores:
        store.wait()


def gate_call(q, k, v, g, eye):
    return pl.pallas_call(
        gate_kernel,
        in_specs=[THERE] * 4 + [HERE],
        out_specs=THERE,
        out_shape=jax.ShapeDtypeStruct((SRC, PAIR, TOK), BF16),
        scratch_shapes=[pltpu.VMEM((TOK, CH), BF16)] * 4
        + [
            pltpu.VMEM((SRC, PAIR, TOK), BF16),
            pltpu.SemaphoreType.DMA((LOADS, 4)),
            pltpu.SemaphoreType.DMA((STORES,)),
        ],
        cost_estimate=pl.CostEstimate(
            flops=4 * 256 * CH * TOK, bytes_accessed=6 * TOK * CH * 2, transcendentals=0
        ),
        name="gate",
    )(q, k, v, g, eye)


def filter_kernel(f_ref, w1_ref, w2_ref, w2l_ref, tc_ref, ts_ref, h_hbm, rows, h_ref, sem):
    for n in range(SRC):
        rows[pl.ds(FS * n, OWN), :] = f_ref[0, :, pl.ds(TOK * n, TOK)]

    def step(c, carry):
        data = rows[pl.ds(c, SRC, stride=FS), :]
        high = data.astype(BF16)
        low = (data - high.astype(F32)).astype(BF16)
        first = mm(w1_ref[...], jnp.concatenate([high, high], 0)) + mm(w1_ref[:, :128], low)
        real, imag = turn_forward(first[:128], first[128:], tc_ref[...], ts_ref[...])
        mid = jnp.concatenate([real, imag], 1)
        mid_high = mid.astype(BF16)
        mid_low = (mid - mid_high.astype(F32)).astype(BF16)
        h_ref[c] = (
            mm(mid_high, w2_ref[...]) + mm(mid_low, w2_ref[...]) + mm(mid_high, w2l_ref[...])
        )
        return carry

    lax.fori_loop(0, OWN, step, 0, unroll=2)
    store = pltpu.make_async_copy(h_ref, h_hbm, sem)
    store.start()
    store.wait()


def filter_call(filt, t):
    tabs = [t[n] for n in ("w1", "w2", "w2l", "tc", "ts")]
    return pl.pallas_call(
        filter_kernel,
        in_specs=[HERE] * (1 + len(tabs)),
        out_specs=THERE,
        out_shape=pltpu.HBM((OWN, 128, 256), F32),
        scratch_shapes=[
            pltpu.VMEM((FS * SRC, TOK), F32),
            pltpu.VMEM((OWN, 128, 256), F32),
            pltpu.SemaphoreType.DMA(()),
        ],
        compiler_params=pltpu.CompilerParams(vmem_limit_bytes=12 << 20),
        cost_estimate=pl.CostEstimate(
            flops=OWN * 5 * 2 * 256 * 256 * 128, bytes_accessed=4 << 20, transcendentals=0
        ),
        name="filter_spectrum",
    )(filt, *tabs)


def conv_kernel(
    x_ref, h_hbm, w1_ref, w2_ref, w4_ref, tc_ref, ts_ref, o_ref, ff_hbm,
    h_ref, ff, xf, of, acc, out, tail, sems, h_sem, ff_sem, *bufs
):
    mid_re, mid_im, prod_re, prod_im, last0, last1, last2 = (
        bufs[GROUP * b : GROUP * b + GROUP] for b in range(7)
    )
    h_loads = []
    for j in range(h_sem.shape[0]):
        rows = pl.ds(2 * GROUP * j, 2 * GROUP)
        h_loads.append(pltpu.make_async_copy(h_hbm.at[rows], h_ref.at[rows], h_sem.at[j]))
        h_loads[j].start()
    for n in range(SRC):
        xf[pl.ds(XS * n, PAIR), :] = x_ref[n].astype(F32)
    acc[...] = jnp.zeros_like(acc)
    steps = OWN // GROUP

    def inverse_outer(c, u):
        last = jnp.concatenate([last0[u][...], last1[u][...], last2[u][...]], 1)
        out = mm(w4_ref[...], last)
        of[pl.ds(c, SRC, stride=XS), :] = out[:, :128]
        of[pl.ds(OWN + c, SRC, stride=XS), :] = out[:, 128:256]
        raw = out[:, 256:]
        ff[pl.ds(c, SRC, stride=FS), :] = raw
        acc[...] += jnp.sum((raw * raw).reshape(SRC // 8, 8, TOK), axis=0)

    def inverse_inner(u):
        tc, ts = tc_ref[...], ts_ref[...]
        back = mm_t(jnp.concatenate([prod_re[u][...], prod_im[u][...]], 1), w2_ref[...])
        for s, last in enumerate((last0[u], last1[u], last2[u])):
            rows = slice(128 * s, 128 * s + 128)
            real, imag = turn_back(back[rows, :128], back[rows, 128:], tc, ts)
            last[:128] = real.astype(BF16)
            last[128:] = imag.astype(BF16)

    def forward_inner(c, u):
        spec = mm(jnp.concatenate([mid_re[u][...], mid_im[u][...]], 1), w2_ref[...])
        kr, ki = spec[:128, :128], spec[:128, 128:]
        gr, gi = spec[128:, :128], spec[128:, 128:]
        hr, hi = h_ref[c, :, :128], h_ref[c, :, 128:]
        prod_re[u][:128] = (kr * hr - ki * hi).astype(BF16)
        prod_im[u][:128] = (kr * hi + ki * hr).astype(BF16)
        prod_re[u][128:256] = (gr * hr + gi * hi).astype(BF16)
        prod_im[u][128:256] = (gi * hr - gr * hi).astype(BF16)
        prod_re[u][256:] = (gr * kr + gi * ki).astype(BF16)
        prod_im[u][256:] = (gi * kr - gr * ki).astype(BF16)

    def forward_outer(c, u):
        tc, ts = tc_ref[...], ts_ref[...]
        kv = xf[pl.ds(c, SRC, stride=XS), :].astype(BF16)
        gg = xf[pl.ds(OWN + c, SRC, stride=XS), :].astype(BF16)
        data = jnp.concatenate([kv, gg], 1)
        first = mm(w1_ref[...], jnp.concatenate([data, data], 0))
        for s in range(2):
            rows = slice(128 * s, 128 * s + 128)
            real, imag = turn_forward(first[:128, rows], first[128:, rows], tc, ts)
            mid_re[u][rows] = real.astype(BF16)
            mid_im[u][rows] = imag.astype(BF16)

    for i in range(steps + 3):
        if 0 <= i - 3 < steps:
            for u in range(GROUP):
                inverse_outer(GROUP * (i - 3) + u, u)
        if 0 <= i - 2 < steps:
            for u in range(GROUP):
                inverse_inner(u)
        if 0 <= i - 1 < steps:
            if (i - 1) % 2 == 0:
                h_loads[(i - 1) // 2].wait()
            for u in range(GROUP):
                forward_inner(GROUP * (i - 1) + u, u)
        if i < steps:
            for u in range(GROUP):
                forward_outer(GROUP * i + u, u)
    ff_store = pltpu.make_async_copy(ff, ff_hbm, ff_sem)
    ff_store.start()
    total = jnp.broadcast_to(jnp.sum(acc[...]), (8, TOK))
    high = total.astype(BF16).astype(F32)
    mid = (total - high).astype(BF16).astype(F32)
    low = total - high - mid
    row = lax.broadcasted_iota(jnp.int32, (2, TOK), 0)
    lane = lax.broadcasted_iota(jnp.int32, (2, TOK), 1)
    high, mid, low = (a[:2] for a in (high, mid, low))
    terms = jnp.where(row == 0, high, jnp.where(lane < 64, mid, low)).astype(BF16)
    tail[...] = jnp.broadcast_to(terms[None, None], tail.shape)
    parts = sems.shape[0] - 1
    tail_store = pltpu.make_async_copy(tail, o_ref.at[:, HALF - 1 :], sems.at[parts])
    tail_store.start()
    stores = []
    for p in range(parts):
        rows = pl.ds(p * (SRC // parts), SRC // parts)
        for n in range(p * (SRC // parts), (p + 1) * (SRC // parts)):
            out[n] = of[pl.ds(XS * n, PAIR), :].astype(BF16)
        there = o_ref.reshape(SRC, ROWS, TOK).at[rows, :PAIR]
        stores.append(pltpu.make_async_copy(out.at[rows], there, sems.at[p]))
        stores[p].start()
    for store in stores:
        store.wait()
    ff_store.wait()
    tail_store.wait()


def conv_call(x, h, t):
    tabs = [t[n] for n in ("w1", "w2", "w4", "tc", "ts")]
    return pl.pallas_call(
        conv_kernel,
        in_specs=[HERE, THERE] + [HERE] * len(tabs),
        out_specs=[THERE, THERE],
        out_shape=(
            jax.ShapeDtypeStruct((SRC, HALF, 2, TOK), BF16),
            pltpu.HBM((SRC * FS, TOK), F32),
        ),
        scratch_shapes=[
            pltpu.VMEM((OWN, 128, 256), F32),
            pltpu.VMEM((SRC * FS, TOK), F32),
            pltpu.VMEM((SRC * XS, TOK), F32),
            pltpu.VMEM((SRC * XS, TOK), F32),
            pltpu.VMEM((8, TOK), F32),
            pltpu.VMEM((SRC, PAIR, TOK), BF16),
            pltpu.VMEM((SRC, 1, 2, TOK), BF16),
            pltpu.SemaphoreType.DMA((5,)),
            pltpu.SemaphoreType.DMA((OWN // (2 * GROUP),)),
            pltpu.SemaphoreType.DMA(()),
        ]
        + [
            pltpu.VMEM((rows, 128), BF16)
            for rows in (256, 256, 384, 384, 256, 256, 256)
            for _ in range(GROUP)
        ],
        compiler_params=pltpu.CompilerParams(vmem_limit_bytes=28 << 20),
        cost_estimate=pl.CostEstimate(
            flops=OWN * 5 * 2 * 256 * 256 * 256, bytes_accessed=6 << 20, transcendentals=0
        ),
        name="conv",
    )(x, h, *tabs)


def arrange_kernel(ff_ref, o_ref):
    for n in range(SRC):
        for b in range(OWN // 8):
            o_ref[pl.ds(8 * b, 8), pl.ds(TOK * n, TOK)] = ff_ref[pl.ds(FS * n + 8 * b, 8), :]


def arrange_call(ff):
    return pl.pallas_call(
        arrange_kernel,
        in_specs=[HERE],
        out_specs=HERE,
        out_shape=jax.ShapeDtypeStruct((OWN, LEN), F32),
        compiler_params=pltpu.CompilerParams(vmem_limit_bytes=8 << 20),
        cost_estimate=pl.CostEstimate(flops=1 << 18, bytes_accessed=2 << 20, transcendentals=0),
        name="arrange",
    )(ff)


def stat_kernel(y_ref, o_ref):
    total = jnp.sum(y_ref[:, HALF - 1, :, :].astype(F32), axis=0)
    total = total[0:1, 0:1] + total[1:2, 0:1] + total[1:2, 64:65]
    o_ref[...] = jnp.broadcast_to(total, (8, TOK))


def stat_call(y):
    return pl.pallas_call(
        stat_kernel,
        in_specs=[HERE],
        out_specs=HERE,
        out_shape=jax.ShapeDtypeStruct((8, TOK), F32),
        compiler_params=pltpu.CompilerParams(vmem_limit_bytes=4 << 20),
        name="stat",
    )(y)


def token_kernel(
    y_ref, k_ref, v_ref, g_ref, eye_ref, qg_ref, kg_ref, vg_ref, qg, kg, vg, sems
):
    eye = eye_ref[:TOK, :TOK]
    stores = []
    for j in range(CHUNKS):
        cols = pl.ds(j * WIDE, WIDE)
        rows = pl.ds(j * GROUPS, GROUPS)
        conv_out = mm_t(eye, y_ref[rows, : OWN // 2].reshape(WIDE, TOK))
        conv_grad = mm_t(eye, y_ref[rows, OWN // 2 : OWN].reshape(WIDE, TOK))
        qg[:, cols] = (g_ref[:, cols].astype(F32) * conv_out).astype(BF16)
        kg[:, cols] = (v_ref[:, cols].astype(F32) * conv_grad).astype(BF16)
        vg[:, cols] = (k_ref[:, cols].astype(F32) * conv_grad).astype(BF16)
        for a, (src, dst) in enumerate(((qg, qg_ref), (kg, kg_ref), (vg, vg_ref))):
            store = pltpu.make_async_copy(src.at[:, cols], dst.at[:, cols], sems.at[j, a])
            store.start()
            stores.append(store)
    for store in stores:
        store.wait()


def token_call(y, k, v, g, eye):
    return pl.pallas_call(
        token_kernel,
        in_specs=[HERE] * 5,
        out_specs=[THERE] * 3,
        out_shape=[jax.ShapeDtypeStruct((TOK, CH), BF16)] * 3,
        scratch_shapes=[pltpu.VMEM((TOK, CH), BF16)] * 3
        + [pltpu.SemaphoreType.DMA((CHUNKS, 3))],
        compiler_params=pltpu.CompilerParams(vmem_limit_bytes=12 << 20),
        cost_estimate=pl.CostEstimate(
            flops=4 * 128 * CH * TOK, bytes_accessed=8 * TOK * CH * 2, transcendentals=0
        ),
        name="token",
    )(y, k, v, g, eye)


def clip_kernel(fr_ref, mine_ref, other_ref, o_ref, buf, sems):
    mean = (mine_ref[0:1, 0:1] + other_ref[0:1, 0:1]) * (1.0 / (D * LEN))
    rms = jnp.sqrt(mean + 1e-6)
    factor = jnp.minimum(1.0, 1.0 / rms)
    factor = jnp.broadcast_to(factor, (OWN, TOK))
    parts = sems.shape[0]
    width = LEN // parts
    copies = []
    for p in range(parts):
        for n in range(width // TOK):
            cols = pl.ds(width * p + TOK * n, TOK)
            buf[:, cols] = fr_ref[:, cols] * factor
        cols = pl.ds(width * p, width)
        copy = pltpu.make_async_copy(buf.at[:, cols], o_ref.at[0, :, cols], sems.at[p])
        copy.start()
        copies.append(copy)
    for copy in copies:
        copy.wait()


def clip_call(fr, mine, other):
    return pl.pallas_call(
        clip_kernel,
        in_specs=[HERE] * 3,
        out_specs=THERE,
        out_shape=jax.ShapeDtypeStruct((1, OWN, LEN), F32),
        scratch_shapes=[pltpu.VMEM((OWN, LEN), F32), pltpu.SemaphoreType.DMA((4,))],
        compiler_params=pltpu.CompilerParams(vmem_limit_bytes=8 << 20),
        cost_estimate=pl.CostEstimate(flops=1 << 18, bytes_accessed=2 << 20, transcendentals=0),
        name="clip",
    )(fr, mine, other)


def exchange(x):
    return lax.all_to_all(x, SEQ_AXES, split_axis=0, concat_axis=0, tiled=True)


def body(query_proj, key_proj, value_proj, output_grad, long_filter):
    t = {name: jnp.asarray(table) for name, table in make_tables().items()}
    sent = gate_call(query_proj, key_proj, value_proj, output_grad, t["eye"])
    arrived = exchange(sent)
    spectrum = filter_call(long_filter, t)
    spectrum = pltpu.with_memory_space_constraint(spectrum, pltpu.HBM)
    back, filter_raw = conv_call(arrived, spectrum, t)
    home = exchange(back)
    placed = arrange_call(filter_raw)
    mine = stat_call(home)
    other = lax.ppermute(mine, "tp", [(0, 1), (1, 0)])
    query_grad, key_grad, value_grad = token_call(
        home, key_proj, value_proj, output_grad, t["eye"]
    )
    filter_grad = clip_call(placed, mine, other)
    return (query_grad, key_grad, value_grad, filter_grad)


def solution(mesh):
    tokens = P(SEQ_AXES, "tp")
    channels = P("tp", SEQ_AXES, None)
    return jax.shard_map(
        body,
        mesh=mesh,
        in_specs=(tokens, tokens, tokens, tokens, channels),
        out_specs=(tokens, tokens, tokens, channels),
        check_vma=False,
    )
```
